128 devices in a mesh: ctx: 16 (over y, x), tp: 8 (over z, core).
Axes of the slice: x: 4, y: 4, z: 4, core: 2. Of those that a mesh axis runs over, the one named last changes fastest.
Arguments:
- ssm_input: bfloat16 [4096, 8192], P('ctx', 'tp'), may hold values from -6 to 6
- dt_raw: float32 [4096, 128], P('ctx', 'tp'), may hold values from -5 to 5
- b_proj: bfloat16 [4096, 8, 256], P('ctx', 'tp'), may hold values from -0.59765625 to 0.59765625
- c_proj: bfloat16 [4096, 8, 256], P('ctx', 'tp'), may hold values from -0.59765625 to 0.59765625
- dt_bias: float32 [128], P('tp'), may hold values from -1.5 to 0.5
- decay_rate: float32 [128], P('tp'), may hold values from 0.0002 to 0.05
- skip_gain: float32 [128], P('tp'), may hold values from 0.5 to 1.5
- doc_start: int32 [4096], P('ctx'), may hold values 0 or 1
- out_weight: bfloat16 [8192, 8192], P('tp'), may hold values from -0.0625 to 0.0625
- grad_out: bfloat16 [4096, 8192], P(('ctx', 'tp')), may hold values from -6 to 6
Outputs:
- layer_out: bfloat16 [4096, 8192], P(('ctx', 'tp'))
- grad_input: bfloat16 [4096, 8192], P('ctx', 'tp')
- grad_dt: float32 [4096, 128], P('ctx', 'tp')
- grad_b: bfloat16 [4096, 8, 256], P('ctx', 'tp')
- grad_c: bfloat16 [4096, 8, 256], P('ctx', 'tp')
- weight_grad: bfloat16 [8192, 8192], P('ctx', 'tp')
The draws below stay inside these ranges and needn't reach their ends.
Inputs may be any that keep to these rules, and one draw needn't show every extreme that they name: `doc_start`: 1 marks the first token of a document; a document runs on until the next 1, across slabs.
All inputs are finite; a program needn't handle non-finite values. No bound on the sum of `doc_start` on one device may be relied on, other than what follows from the above.
Results may differ from the reference program's by a relative error of at most 0.022.
Values may be sent and summed in bfloat16 or wider, within the bound.
No kernel may reach another device: no remote copies, remote signals or barrier semaphores. Data moves between devices by JAX's collectives and lax.ppermute only.
A program may use at most 256 MiB of HBM per device.

```python
import math
import jax
import jax.numpy as jnp
from jax import lax

WIDTH = 8192
HEADS_DEV = 16
HEAD_DIM = 64
STATE = 256
TOK_DEV = 256
GROUPS = 8
HEADS = 128
INNER = 8192
TOKENS = 4096
N_CTX = 16


def touch_ends(array, rng, smallest, high):
    extent = array.shape
    place = [jax.random.randint(jax.random.fold_in(rng, axis), (), 0, extent[axis]) for axis in range(len(extent))]
    array = array.at[tuple(place)].set(smallest)
    longest = extent.index(max(extent))
    place[longest] = (place[longest] + 1) % extent[longest]
    return array.at[tuple(place)].set(high)


def shard_levels(rng, extent, split, low, top_value):
    level = 1.0
    for axis_at, shards_of in split:
        draws = jax.random.uniform(jax.random.fold_in(jax.random.fold_in(rng, 6), axis_at), (shards_of,), jnp.float32, low / len(split), top_value / len(split))
        level = level * jnp.repeat(jnp.exp(draws), extent[axis_at] // shards_of).reshape((-1,) + (1,) * (len(extent) - 1 - axis_at))
    return level


def centred(key, dims, spread, bound, cuts=(), dtype=jnp.bfloat16):
    factor_of = shard_levels(key, dims, cuts, -0.22, 0.18) if cuts else 1.0
    array = jax.random.normal(key, dims, jnp.float32) * spread * factor_of
    return jnp.minimum(jnp.maximum(array, -bound), bound).astype(dtype)


def setup_inputs(seed: int = 0) -> dict:
    splits = jax.random.split(jax.random.key(seed), 11)
    return {
        "ssm_input": centred(splits[0], (TOKENS, INNER), 1.0, 6.0, ((0, 16), (1, 8))),
        "dt_raw": centred(splits[1], (TOKENS, HEADS), 1.0, 5.0, ((0, 16), (1, 8)), jnp.float32),
        "b_proj": centred(splits[2], (TOKENS, GROUPS, STATE), 0.1, 0.59765625, ((0, 16), (1, 8))),
        "c_proj": centred(splits[3], (TOKENS, GROUPS, STATE), 0.1, 0.59765625, ((0, 16), (1, 8))),
        "dt_bias": jnp.clip(-1.5 + 2.0 * jax.random.uniform(splits[4], (HEADS,), jnp.float32) ** shard_levels(splits[4], (HEADS,), ((0, 8),), -0.2, 0.2), -1.5, 0.5),
        "decay_rate": jnp.clip(jnp.exp(math.log(0.05) - 5.521461 * jax.random.uniform(splits[5], (HEADS,), jnp.float32) ** shard_levels(splits[5], (HEADS,), ((0, 8),), -0.2, 0.2)), 0.0002, 0.05),
        "skip_gain": jnp.clip(1.0 + 0.1 * jax.random.normal(splits[6], (HEADS,), jnp.float32), 0.5, 1.5),
        "doc_start": touch_ends((jax.random.randint(splits[7], (TOKENS,), 0, 4096) < 1).astype(jnp.int32), jax.random.fold_in(splits[7], 1), 0, 1),
        "out_weight": centred(splits[8], (INNER, WIDTH), INNER ** -0.5, 0.0625, ((0, 8),)),
        "grad_out": centred(splits[9], (TOKENS, WIDTH), 1.0, 6.0, ((0, 128),)),
    }


HIGHEST = lax.Precision.HIGHEST

def block_ssd(seq_in, step_raw, b_rows, c_rows, carried, doc_start, bias_heads, rate_heads, skip_heads):
    length = seq_in.shape[0]
    step_size = jax.nn.softplus(step_raw + bias_heads)
    cumul = jnp.cumsum(-step_size * rate_heads, axis=0)
    segment = jnp.cumsum(doc_start)
    reach = (segment == 0).astype(jnp.float32)
    order = jnp.arange(length)
    causal = (segment[:, None] == segment[None, :]) & (order[:, None] >= order[None, :])
    cum_heads = jnp.transpose(cumul, (1, 2, 0))
    differ = cum_heads[:, :, :, None] - cum_heads[:, :, None, :]
    decays = jnp.exp(jnp.where(causal, differ, -jnp.inf))
    scores = jnp.einsum('tgn,sgn->gts', c_rows, b_rows)
    mixing = decays * scores[:, None] * jnp.transpose(step_size, (1, 2, 0))[:, :, None, :]
    inside = jnp.einsum('gkts,sgkp->tgkp', mixing, seq_in, precision=HIGHEST)
    entry = jnp.exp(cumul) * reach[:, None, None]
    from_carry = entry[..., None] * jnp.einsum('tgn,gkpn->tgkp', c_rows, carried, precision=HIGHEST)
    mixer = inside + from_carry + skip_heads[..., None] * seq_in
    same_last = (segment == segment[-1]).astype(jnp.float32)
    tail = jnp.exp(cumul[-1] - cumul) * same_last[:, None, None] * step_size
    local_state = jnp.einsum('sgk,sgkp,sgn->gkpn', tail, seq_in, b_rows, precision=HIGHEST)
    through = reach[-1] * jnp.exp(cumul[-1])
    return (mixer, local_state, through)

def reference(ssm_input, dt_raw, b_proj, c_proj, dt_bias, decay_rate, skip_gain, doc_start, out_weight, grad_out):
    bias_heads = dt_bias.reshape(GROUPS, HEADS_DEV)
    rate_heads = decay_rate.reshape(GROUPS, HEADS_DEV)
    skip_heads = skip_gain.reshape(GROUPS, HEADS_DEV)
    starts = doc_start.reshape(N_CTX, TOK_DEV)
    block_fn = jax.checkpoint(block_ssd)

    def forward(seq_all, step_all, b_all, c_all):
        seq_blocks = seq_all.reshape(N_CTX, TOK_DEV, GROUPS, HEADS_DEV, HEAD_DIM)
        step_blocks = step_all.reshape(N_CTX, TOK_DEV, GROUPS, HEADS_DEV)
        b_blocks = b_all.reshape(N_CTX, TOK_DEV, GROUPS, STATE)
        c_blocks = c_all.reshape(N_CTX, TOK_DEV, GROUPS, STATE)

        def advance(carried, pieces):
            mixer, local_state, through = block_fn(pieces[0], pieces[1], pieces[2], pieces[3], carried, pieces[4], bias_heads, rate_heads, skip_heads)
            return (through[..., None, None] * carried + local_state, mixer)
        start_state = jnp.zeros((GROUPS, HEADS_DEV, HEAD_DIM, STATE), jnp.float32)
        _, mixers = lax.scan(advance, start_state, (seq_blocks, step_blocks, b_blocks, c_blocks, starts))
        return mixers.reshape(TOKENS, INNER)
    mixer_all, pullback = jax.vjp(forward, ssm_input.astype(jnp.float32), dt_raw, b_proj.astype(jnp.float32), c_proj.astype(jnp.float32))
    mixer_bf = mixer_all.astype(jnp.bfloat16)
    panels = jnp.transpose(mixer_bf.reshape(TOKENS, GROUPS, HEADS_DEV * HEAD_DIM), (1, 0, 2))
    weight_panels = out_weight.reshape(GROUPS, HEADS_DEV * HEAD_DIM, WIDTH)

    def add_panel(total, pair):
        partial_sum = jnp.dot(pair[0], pair[1], preferred_element_type=jnp.float32).astype(jnp.bfloat16)
        partial_sum = lax.optimization_barrier(partial_sum)
        return (total + partial_sum.astype(jnp.float32), None)
    out_sum, _ = lax.scan(add_panel, jnp.zeros((TOKENS, WIDTH), jnp.float32), (panels, weight_panels))
    layer_out = out_sum.astype(jnp.bfloat16)
    grad_mix = lax.dot_general(grad_out, out_weight, (((1,), (1,)), ((), ())), preferred_element_type=jnp.float32).astype(jnp.bfloat16)
    grad_seq, grad_step, grad_brows, grad_crows = pullback(grad_mix.astype(jnp.float32))
    weight_grad = lax.dot_general(grad_out, mixer_bf, (((0,), (0,)), ((), ())), preferred_element_type=jnp.float32).astype(jnp.bfloat16)
    return (layer_out, grad_seq.astype(jnp.bfloat16), grad_step, grad_brows.astype(jnp.bfloat16), grad_crows.astype(jnp.bfloat16), weight_grad)
```

```python
import jax
import jax.numpy as jnp
from jax import lax
from jax.experimental import pallas as pl
from jax.experimental.pallas import tpu as pltpu
from jax.sharding import PartitionSpec as P

F32 = jnp.float32
BF16 = jnp.bfloat16
HIGHEST = lax.Precision.HIGHEST
ROWS = 256
HEADS = 16
DIM = 64
STATE = 256
WIDE = HEADS * DIM
PAIRS = HEADS // 2
EXTRA = 8
MASKED = -1e30
CUM, STEP, ENTRY, ETAIL, TAIL, THROUGH, SEG, SIG = range(8)


def dot(a, b, dims, precision=None):
    return lax.dot_general(a, b, (dims, ((), ())), precision=precision, preferred_element_type=F32)


def nn(a, b):
    return dot(a, b, ((1,), (0,)))


def nt(a, b):
    return dot(a, b, ((1,), (1,)))


def tn(a, b):
    return dot(a, b, ((0,), (0,)))


def vmem(n):
    return [pl.BlockSpec(memory_space=pltpu.VMEM)] * n


def smem(n):
    return [pl.BlockSpec(memory_space=pltpu.SMEM)] * n


def params():
    return pltpu.CompilerParams(vmem_limit_bytes=48 * 1024 * 1024)


def iota(shape, axis):
    return lax.broadcasted_iota(jnp.int32, shape, axis)


def col(tab, which, head):
    at = which * HEADS + head
    return tab[:, at : at + 1]


def pair_cols(tab, which, pair):
    low = iota((ROWS, 2 * DIM), 1) < DIM
    return jnp.where(low, col(tab, which, 2 * pair), col(tab, which, 2 * pair + 1))


def cols_of(pair):
    return slice(pair * 2 * DIM, (pair + 1) * 2 * DIM)


def states_kernel(bias, rate, x, dt, doc, b, payload, tab_rows, tab_cols):
    head = iota((HEADS, ROWS), 0)
    bias_rows = jnp.zeros((HEADS, ROWS), F32)
    rate_rows = jnp.zeros((HEADS, ROWS), F32)
    for h in range(HEADS):
        bias_rows = jnp.where(head == h, bias[h], bias_rows)
        rate_rows = jnp.where(head == h, rate[h], rate_rows)
    raw = dt[...] + bias_rows
    small = jnp.exp(-jnp.abs(raw))
    step = jnp.maximum(raw, 0.0) + jnp.log1p(small)
    sig = jnp.where(raw >= 0, 1.0, small) / (1.0 + small)
    upto = (iota((ROWS, ROWS), 0) <= iota((ROWS, ROWS), 1)).astype(F32)
    cum = dot(-step * rate_rows, upto, ((1,), (0,)), HIGHEST)
    starts = jnp.broadcast_to(doc[...].astype(F32), (HEADS, ROWS))
    seg = nn(starts.astype(BF16), upto.astype(BF16))
    last = cum[:, ROWS - 1 :]
    seg_last = seg[:, ROWS - 1 :]
    entry = jnp.where(seg == 0.0, jnp.exp(cum), 0.0)
    etail = jnp.where(seg == seg_last, jnp.exp(last - cum), 0.0)
    through = jnp.broadcast_to(jnp.where(seg_last == 0.0, jnp.exp(last), 0.0), (HEADS, ROWS))
    rows = jnp.concatenate([cum, step, entry, etail, etail * step, through, seg, sig], axis=0)
    tab_rows[...] = rows
    tab = rows.T
    tab_cols[...] = tab
    for j in range(PAIRS):
        weighted = (x[:, cols_of(j)].astype(F32) * pair_cols(tab, TAIL, j)).astype(BF16)
        state = tn(weighted, b[...]).astype(BF16)
        payload[2 * j, :DIM, :] = state[:DIM]
        payload[2 * j + 1, :DIM, :] = state[DIM:]
    upper = through.astype(BF16).astype(F32)
    lower = through - upper
    which = iota((EXTRA, ROWS), 0)
    for h in range(HEADS):
        tail_rows = jnp.where(which == 0, upper[h : h + 1], jnp.where(which == 1, lower[h : h + 1], 0.0))
        payload[h, DIM:, :] = tail_rows.astype(BF16)


def states(bias, rate, x, dt, doc, b):
    return pl.pallas_call(
        states_kernel,
        in_specs=smem(2) + vmem(4),
        out_specs=vmem(3),
        out_shape=(
            jax.ShapeDtypeStruct((HEADS, DIM + EXTRA, STATE), BF16),
            jax.ShapeDtypeStruct((8 * HEADS, ROWS), F32),
            jax.ShapeDtypeStruct((ROWS, 8 * HEADS), F32),
        ),
        compiler_params=params(),
    )(bias, rate, x, dt, doc, b)


def prefix_kernel(got, out, decay):
    slabs = got.shape[0]
    carry = jnp.zeros((DIM, STATE), F32)
    for c in range(slabs):
        out[c] = carry.astype(BF16)
        extra = got[c, DIM:, :].astype(F32)
        through = extra[0:1] + extra[1:2]
        decay[c : c + 1, :] = through
        carry = through * carry + got[c, :DIM, :].astype(F32)


def prefix(got):
    slabs = got.shape[0]
    return pl.pallas_call(
        prefix_kernel,
        in_specs=vmem(1),
        out_specs=vmem(2),
        out_shape=(
            jax.ShapeDtypeStruct((slabs, DIM, STATE), BF16),
            jax.ShapeDtypeStruct((slabs, STATE), F32),
        ),
        compiler_params=params(),
    )(got)


def suffix_kernel(got, decay, out):
    slabs = got.shape[0]
    carry = jnp.zeros((DIM, STATE), F32)
    for c in reversed(range(slabs)):
        out[c] = carry.astype(BF16)
        carry = decay[c : c + 1, :] * carry + got[c].astype(F32)


def suffix(got, decay):
    return pl.pallas_call(
        suffix_kernel,
        in_specs=vmem(2),
        out_specs=vmem(1)[0],
        out_shape=jax.ShapeDtypeStruct(got.shape, BF16),
        compiler_params=params(),
    )(got, decay)


def mixer_kernel(skip, x, b, c, rows, tab_ref, carried, mixed, inner):
    tab = tab_ref[...]
    scores = nt(c[...], b[...])
    order_t, order_s = iota((ROWS, ROWS), 0), iota((ROWS, ROWS), 1)
    seg_row = rows[SEG * HEADS : SEG * HEADS + 1, :]
    mask = jnp.where((order_t >= order_s) & (col(tab, SEG, 0) == seg_row), 0.0, MASKED)
    low = iota((ROWS, 2 * DIM), 1) < DIM
    for j in range(PAIRS):
        x_pair = x[:, cols_of(j)].astype(F32)
        scaled = (x_pair * pair_cols(tab, STEP, j)).astype(BF16)
        parts = []
        for h in (2 * j, 2 * j + 1):
            row = rows[CUM * HEADS + h : CUM * HEADS + h + 1, :]
            weight = jnp.exp(col(tab, CUM, h) - row + mask) * scores
            parts.append(nn(weight.astype(BF16), scaled))
        state = carried[2 * j : 2 * j + 2].reshape(2 * DIM, STATE)
        got = jnp.where(low, parts[0], parts[1]) + pair_cols(tab, ENTRY, j) * nt(c[...], state)
        inner[:, cols_of(j)] = got
        gain = jnp.where(low, skip[2 * j], skip[2 * j + 1])
        mixed[:, cols_of(j)] = (got + gain * x_pair).astype(BF16)


def mixer(skip, x, b, c, rows, tab, carried):
    return pl.pallas_call(
        mixer_kernel,
        in_specs=smem(1) + vmem(6),
        out_specs=vmem(2),
        out_shape=(
            jax.ShapeDtypeStruct((ROWS, WIDE), BF16),
            jax.ShapeDtypeStruct((ROWS, WIDE), F32),
        ),
        compiler_params=params(),
    )(skip, x, b, c, rows, tab, carried)


def local_grad_kernel(grad, c, tab_ref, out):
    tab = tab_ref[...]
    for j in range(PAIRS):
        weighted = (grad[:, cols_of(j)].astype(F32) * pair_cols(tab, ENTRY, j)).astype(BF16)
        state = tn(weighted, c[...]).astype(BF16)
        out[2 * j] = state[:DIM]
        out[2 * j + 1] = state[DIM:]


def local_grad(grad, c, tab):
    return pl.pallas_call(
        local_grad_kernel,
        in_specs=vmem(3),
        out_specs=vmem(1)[0],
        out_shape=jax.ShapeDtypeStruct((HEADS, DIM, STATE), BF16),
        compiler_params=params(),
    )(grad, c, tab)


def head_sums(pair, values):
    head = iota((HEADS, 2 * DIM), 0)
    own = (head == 2 * pair + iota((HEADS, 2 * DIM), 1) // DIM).astype(BF16)
    upper = values.astype(BF16)
    lower = (values - upper.astype(F32)).astype(BF16)
    return nt(own, upper) + nt(own, lower)


def backward_kernel(
    skip, rate, x, b, c, rows, tab_ref, carried, inner, grad, after, grad_x, grad_dt, grad_b, grad_c
):
    tab = tab_ref[...]
    scores = nt(b[...], c[...])
    order_s, order_t = iota((ROWS, ROWS), 0), iota((ROWS, ROWS), 1)
    seg_row = rows[SEG * HEADS : SEG * HEADS + 1, :]
    mask = jnp.where((order_t >= order_s) & (col(tab, SEG, 0) == seg_row), 0.0, MASKED)
    low = iota((ROWS, 2 * DIM), 1) < DIM
    grad_scores = jnp.zeros((ROWS, ROWS), F32)
    b_sum = jnp.zeros((ROWS, STATE), F32)
    c_sum = jnp.zeros((ROWS, STATE), F32)
    step_grad = jnp.zeros((HEADS, ROWS), F32)
    cum_grad = jnp.zeros((HEADS, ROWS), F32)
    state_dot = jnp.zeros((HEADS, ROWS), F32)
    tail_dot = jnp.zeros((HEADS, ROWS), F32)
    for j in range(PAIRS):
        x_pair = x[:, cols_of(j)].astype(F32)
        step = pair_cols(tab, STEP, j)
        scaled_f = x_pair * step
        scaled = scaled_f.astype(BF16)
        g = grad[:, cols_of(j)]
        g_f = g.astype(F32)
        zero = jnp.zeros_like(g)
        parts = []
        for k in range(2):
            h = 2 * j + k
            row = rows[CUM * HEADS + h : CUM * HEADS + h + 1, :]
            decay = jnp.exp(row - col(tab, CUM, h) + mask)
            own = jnp.where(low if k == 0 else jnp.logical_not(low), g, zero)
            grad_scores = grad_scores + nt(scaled, own) * decay
            parts.append(nn((decay * scores).astype(BF16), g))
        nxt = after[2 * j : 2 * j + 2].reshape(2 * DIM, STATE)
        prev = carried[2 * j : 2 * j + 2].reshape(2 * DIM, STATE)
        etail = pair_cols(tab, ETAIL, j)
        from_tail = etail * nt(b[...], nxt)
        total = jnp.where(low, parts[0], parts[1]) + from_tail
        gain = jnp.where(low, skip[2 * j], skip[2 * j + 1])
        grad_x[:, cols_of(j)] = (step * total + gain * g_f).astype(BF16)
        step_grad = step_grad + head_sums(j, x_pair * total)
        cum_grad = cum_grad + head_sums(j, g_f * inner[:, cols_of(j)])
        tail_dot = tail_dot + head_sums(j, scaled_f * from_tail)
        product = nxt.astype(F32) * prev.astype(F32)
        head = iota((HEADS, 2 * DIM), 0)
        own_rows = (head == 2 * j + iota((HEADS, 2 * DIM), 1) // DIM).astype(BF16)
        upper = product.astype(BF16)
        lower = (product - upper.astype(F32)).astype(BF16)
        state_dot = state_dot + nn(own_rows, upper) + nn(own_rows, lower)
        b_sum = b_sum + nn((etail * scaled_f).astype(BF16), nxt)
        c_sum = c_sum + nn((pair_cols(tab, ENTRY, j) * g_f).astype(BF16), prev)
    flow = grad_scores.astype(BF16)
    grad_b[...] = (b_sum + nn(flow, c[...])).astype(BF16)
    grad_c[...] = (c_sum + tn(flow, b[...])).astype(BF16)
    step_rows = rows[STEP * HEADS : (STEP + 1) * HEADS, :]
    through = rows[THROUGH * HEADS : (THROUGH + 1) * HEADS, :]
    end = jnp.sum(tail_dot, axis=1, keepdims=True) + jnp.sum(
        through * state_dot, axis=1, keepdims=True
    )
    cum_grad = cum_grad - step_rows * step_grad
    since = (iota((ROWS, ROWS), 0) >= iota((ROWS, ROWS), 1)).astype(F32)
    decay_grad = dot(cum_grad, since, ((1,), (0,)), HIGHEST) + end
    head = iota((HEADS, ROWS), 0)
    rate_rows = jnp.zeros((HEADS, ROWS), F32)
    for h in range(HEADS):
        rate_rows = jnp.where(head == h, rate[h], rate_rows)
    sig = rows[SIG * HEADS : (SIG + 1) * HEADS, :]
    grad_dt[...] = (step_grad - rate_rows * decay_grad) * sig


def backward(skip, rate, x, b, c, rows, tab, carried, inner, grad, after):
    return pl.pallas_call(
        backward_kernel,
        in_specs=smem(2) + vmem(9),
        out_specs=vmem(4),
        out_shape=(
            jax.ShapeDtypeStruct((ROWS, WIDE), BF16),
            jax.ShapeDtypeStruct((HEADS, ROWS), F32),
            jax.ShapeDtypeStruct((ROWS, STATE), BF16),
            jax.ShapeDtypeStruct((ROWS, STATE), BF16),
        ),
        compiler_params=params(),
    )(skip, rate, x, b, c, rows, tab, carried, inner, grad, after)


def weight_kernel(core, own, other, mixed, out, acc):
    at = pl.program_id(0)

    @pl.when(at == 0)
    def _():
        acc[...] = jnp.zeros_like(acc)

    mine = core[0]
    slabs, planes, _, share, wide = mixed.shape
    total = None
    for source, which in ((own, mine), (other, 1 - mine)):
        left = jnp.concatenate(
            [source[z, k * share : (k + 1) * share] for k in range(slabs) for z in range(planes)], 0
        )
        right = jnp.concatenate(
            [mixed[k, z, which] for k in range(slabs) for z in range(planes)], 0
        )
        part = tn(left, right)
        total = part if total is None else total + part
    acc[...] += total

    @pl.when(at == pl.num_programs(0) - 1)
    def _():
        out[...] = acc[...].astype(BF16)


def weight_grad(core, own, other, mixed):
    planes, spread, cols = own.shape
    slabs, _, _, share, wide = mixed.shape
    block = 2
    return pl.pallas_call(
        weight_kernel,
        grid=(slabs // block,),
        in_specs=[
            pl.BlockSpec(memory_space=pltpu.SMEM),
            pl.BlockSpec((planes, block * share, cols), lambda i: (0, i, 0)),
            pl.BlockSpec((planes, block * share, cols), lambda i: (0, i, 0)),
            pl.BlockSpec((block, planes, 2, share, wide), lambda i: (i, 0, 0, 0, 0)),
        ],
        out_specs=pl.BlockSpec((cols, wide), lambda i: (0, 0)),
        out_shape=jax.ShapeDtypeStruct((cols, wide), BF16),
        scratch_shapes=[pltpu.VMEM((cols, wide), F32)],
        compiler_params=params(),
    )(core, own, other, mixed)


SWAP = [(i, i ^ 1) for i in range(8)]
PLANES = [[0, 2, 4, 6], [1, 3, 5, 7]]


def over_planes(value):
    return lax.all_to_all(value, "tp", 0, 0, tiled=True, axis_index_groups=PLANES)


def shards(
    ssm_input,
    dt_raw,
    b_proj,
    c_proj,
    dt_bias,
    decay_rate,
    skip_gain,
    doc_start,
    out_weight,
    grad_out,
):
    share, width = grad_out.shape
    n_ctx = lax.axis_size("ctx")
    n_tp = lax.axis_size("tp")
    core = lax.axis_index("tp") % 2
    b = b_proj.reshape(ROWS, STATE)
    c = c_proj.reshape(ROWS, STATE)
    grad_full = lax.all_gather(grad_out, "tp", axis=0, tiled=True)
    payload, rows, tab = states(
        dt_bias, decay_rate, ssm_input, dt_raw.T, doc_start.reshape(1, ROWS), b
    )
    carried, decay = prefix(lax.all_to_all(payload, "ctx", 0, 0, tiled=True))
    carried = lax.all_to_all(carried, "ctx", 0, 0, tiled=True)
    mixed, inner = mixer(skip_gain, ssm_input, b, c, rows, tab, carried)

    mixed_all = lax.all_gather(mixed, "ctx", axis=0, tiled=True)
    columns = lax.all_to_all(grad_out, "ctx", 1, 0, tiled=True)
    own = over_planes(jnp.broadcast_to(columns, (4,) + columns.shape))
    other = lax.ppermute(own, "tp", SWAP)

    partial = nn(mixed, out_weight).astype(BF16).reshape(n_tp // 2, 2, share, width)
    keep = lax.dynamic_index_in_dim(partial, core, 1, False)
    send = lax.dynamic_index_in_dim(partial, 1 - core, 1, False)
    both = keep.astype(F32) + lax.ppermute(send, "tp", SWAP).astype(F32)
    layer_out = jnp.sum(over_planes(both.astype(BF16)).astype(F32), axis=0).astype(BF16)

    grad_mix = nt(grad_full, out_weight).astype(BF16)
    after = suffix(
        lax.all_to_all(local_grad(grad_mix, c, tab), "ctx", 0, 0, tiled=True), decay
    )
    after = lax.all_to_all(after, "ctx", 0, 0, tiled=True)
    grad_x, grad_dt, grad_b, grad_c = backward(
        skip_gain, decay_rate, ssm_input, b, c, rows, tab, carried, inner, grad_mix, after
    )
    weight = weight_grad(
        core.reshape(1),
        own,
        other,
        mixed_all.reshape(n_ctx, n_tp // 2, 2, share, WIDE),
    )
    return (
        layer_out,
        grad_x,
        grad_dt.T,
        grad_b.reshape(ROWS, 1, STATE),
        grad_c.reshape(ROWS, 1, STATE),
        weight,
    )


def solution(mesh):
    in_specs = (
        P("ctx", "tp"),
        P("ctx", "tp"),
        P("ctx", "tp", None),
        P("ctx", "tp", None),
        P("tp"),
        P("tp"),
        P("tp"),
        P("ctx"),
        P("tp", None),
        P(("ctx", "tp"), None),
    )
    out_specs = (
        P(("ctx", "tp"), None),
        P("ctx", "tp"),
        P("ctx", "tp"),
        P("ctx", "tp", None),
        P("ctx", "tp", None),
        P("ctx", "tp"),
    )
    return jax.shard_map(shards, mesh=mesh, in_specs=in_specs, out_specs=out_specs, check_vma=False)
```

```python
import jax
import jax.numpy as jnp
from jax import lax
from jax.experimental import pallas as pl
from jax.experimental.pallas import tpu as pltpu
from jax.sharding import PartitionSpec as P

F32 = jnp.float32
BF16 = jnp.bfloat16
HIGHEST = lax.Precision.HIGHEST
ROWS = 256
HEADS = 16
DIM = 64
STATE = 256
WIDE = HEADS * DIM
PAIRS = HEADS // 2
EXTRA = 8
MASKED = -1e30
CUM, STEP, ENTRY, ETAIL, TAIL, THROUGH, SEG, SIG = range(8)


def dot(a, b, dims, precision=None):
    return lax.dot_general(a, b, (dims, ((), ())), precision=precision, preferred_element_type=F32)


def nn(a, b):
    return dot(a, b, ((1,), (0,)))


def nt(a, b):
    return dot(a, b, ((1,), (1,)))


def tn(a, b):
    return dot(a, b, ((0,), (0,)))


def smem(n):
    return [pl.BlockSpec(memory_space=pltpu.SMEM)] * n


def hbm(n):
    return [pl.BlockSpec(memory_space=pltpu.HBM)] * n


def pinned(*arrays):
    return [pltpu.with_memory_space_constraint(a, pltpu.HBM) for a in arrays]


def staged(kernel, scalars, arrays, outs):
    given = list(scalars) + list(arrays)
    n, m = len(given), len(outs)

    def body(*refs):
        sources, results, local, sems = refs[:n], refs[n : n + m], refs[n + m : -1], refs[-1]
        copies = [
            pltpu.make_async_copy(a, b, sems.at[i])
            for i, (a, b) in enumerate(zip(sources, local[:n], strict=True))
        ]
        for copy in copies:
            copy.start()
        for copy in copies:
            copy.wait()
        kernel(*local)
        copies = [
            pltpu.make_async_copy(a, b, sems.at[n + i])
            for i, (a, b) in enumerate(zip(local[n:], results, strict=True))
        ]
        for copy in copies:
            copy.start()
        for copy in copies:
            copy.wait()

    return pl.pallas_call(
        body,
        in_specs=hbm(n),
        out_specs=hbm(m),
        out_shape=tuple(jax.ShapeDtypeStruct(*out) for out in outs),
        scratch_shapes=[pltpu.SMEM(a.shape, a.dtype) for a in scalars]
        + [pltpu.VMEM(a.shape, a.dtype) for a in arrays]
        + [pltpu.VMEM(*out) for out in outs]
        + [pltpu.SemaphoreType.DMA((n + m,))],
        compiler_params=params(),
    )(*given)


def params():
    return pltpu.CompilerParams(vmem_limit_bytes=32 * 1024 * 1024)


def iota(shape, axis):
    return lax.broadcasted_iota(jnp.int32, shape, axis)


def col(tab, which, head):
    at = which * HEADS + head
    return tab[:, at : at + 1]


def pair_cols(tab, which, pair):
    low = iota((ROWS, 2 * DIM), 1) < DIM
    return jnp.where(low, col(tab, which, 2 * pair), col(tab, which, 2 * pair + 1))


def cols_of(pair):
    return slice(pair * 2 * DIM, (pair + 1) * 2 * DIM)


def states_kernel(bias, rate, x, dt, doc, b, payload, tab_rows, tab_cols):
    head = iota((HEADS, ROWS), 0)
    bias_rows = jnp.zeros((HEADS, ROWS), F32)
    rate_rows = jnp.zeros((HEADS, ROWS), F32)
    for h in range(HEADS):
        bias_rows = jnp.where(head == h, bias[h], bias_rows)
        rate_rows = jnp.where(head == h, rate[h], rate_rows)
    raw = dt[...] + bias_rows
    small = jnp.exp(-jnp.abs(raw))
    step = jnp.maximum(raw, 0.0) + jnp.log1p(small)
    sig = jnp.where(raw >= 0, 1.0, small) / (1.0 + small)
    upto = (iota((ROWS, ROWS), 0) <= iota((ROWS, ROWS), 1)).astype(F32)
    cum = dot(-step * rate_rows, upto, ((1,), (0,)), HIGHEST)
    starts = jnp.broadcast_to(doc[...].astype(F32), (HEADS, ROWS))
    seg = nn(starts.astype(BF16), upto.astype(BF16))
    last = cum[:, ROWS - 1 :]
    seg_last = seg[:, ROWS - 1 :]
    entry = jnp.where(seg == 0.0, jnp.exp(cum), 0.0)
    etail = jnp.where(seg == seg_last, jnp.exp(last - cum), 0.0)
    through = jnp.broadcast_to(jnp.where(seg_last == 0.0, jnp.exp(last), 0.0), (HEADS, ROWS))
    rows = jnp.concatenate([cum, step, entry, etail, etail * step, through, seg, sig], axis=0)
    tab_rows[...] = rows
    tab = rows.T
    tab_cols[...] = tab
    for j in range(PAIRS):
        weighted = (x[:, cols_of(j)].astype(F32) * pair_cols(tab, TAIL, j)).astype(BF16)
        state = tn(weighted, b[...]).astype(BF16)
        payload[2 * j, :DIM, :] = state[:DIM]
        payload[2 * j + 1, :DIM, :] = state[DIM:]
    upper = through.astype(BF16).astype(F32)
    lower = through - upper
    which = iota((EXTRA, ROWS), 0)
    for h in range(HEADS):
        tail_rows = jnp.where(which == 0, upper[h : h + 1], jnp.where(which == 1, lower[h : h + 1], 0.0))
        payload[h, DIM:, :] = tail_rows.astype(BF16)


def states(bias, rate, x, dt, doc, b):
    outs = [
        ((HEADS, DIM + EXTRA, STATE), BF16),
        ((8 * HEADS, ROWS), F32),
        ((ROWS, 8 * HEADS), F32),
    ]
    return staged(states_kernel, (bias, rate), (x, dt, doc, b), outs)


def prefix_kernel(got, out, decay):
    slabs = got.shape[0]
    carry = jnp.zeros((DIM, STATE), F32)
    for c in range(slabs):
        out[c] = carry.astype(BF16)
        extra = got[c, DIM:, :].astype(F32)
        through = extra[0:1] + extra[1:2]
        decay[c : c + 1, :] = through
        carry = through * carry + got[c, :DIM, :].astype(F32)


def prefix(got):
    slabs = got.shape[0]
    outs = [((slabs, DIM, STATE), BF16), ((slabs, STATE), F32)]
    return staged(prefix_kernel, (), (got,), outs)


def suffix_kernel(got, decay, out):
    slabs = got.shape[0]
    carry = jnp.zeros((DIM, STATE), F32)
    for c in reversed(range(slabs)):
        out[c] = carry.astype(BF16)
        carry = decay[c : c + 1, :] * carry + got[c].astype(F32)


def suffix(got, decay):
    return staged(suffix_kernel, (), (got, decay), [(got.shape, BF16)])[0]


def mixer_kernel(skip, x, b, c, rows, tab_ref, carried, mixed, inner):
    tab = tab_ref[...]
    scores = nt(c[...], b[...])
    order_t, order_s = iota((ROWS, ROWS), 0), iota((ROWS, ROWS), 1)
    seg_row = rows[SEG * HEADS : SEG * HEADS + 1, :]
    mask = jnp.where((order_t >= order_s) & (col(tab, SEG, 0) == seg_row), 0.0, MASKED)
    low = iota((ROWS, 2 * DIM), 1) < DIM
    for j in range(PAIRS):
        x_pair = x[:, cols_of(j)].astype(F32)
        scaled = (x_pair * pair_cols(tab, STEP, j)).astype(BF16)
        parts = []
        for h in (2 * j, 2 * j + 1):
            row = rows[CUM * HEADS + h : CUM * HEADS + h + 1, :]
            weight = jnp.exp(col(tab, CUM, h) - row + mask) * scores
            parts.append(nn(weight.astype(BF16), scaled))
        state = carried[2 * j : 2 * j + 2].reshape(2 * DIM, STATE)
        got = jnp.where(low, parts[0], parts[1]) + pair_cols(tab, ENTRY, j) * nt(c[...], state)
        inner[:, cols_of(j)] = got
        gain = jnp.where(low, skip[2 * j], skip[2 * j + 1])
        mixed[:, cols_of(j)] = (got + gain * x_pair).astype(BF16)


def mixer(skip, x, b, c, rows, tab, carried):
    outs = [((ROWS, WIDE), BF16), ((ROWS, WIDE), F32)]
    return staged(mixer_kernel, (skip,), (x, b, c, rows, tab, carried), outs)


def head_sums(pair, values):
    head = iota((HEADS, 2 * DIM), 0)
    own = (head == 2 * pair + iota((HEADS, 2 * DIM), 1) // DIM).astype(BF16)
    upper = values.astype(BF16)
    lower = (values - upper.astype(F32)).astype(BF16)
    return nt(own, upper) + nt(own, lower)


def backward_kernel(
    skip, rate, x, b, c, rows, tab_ref, carried, inner, grad, after, grad_x, grad_dt, grad_b, grad_c
):
    tab = tab_ref[...]
    scores = nt(b[...], c[...])
    order_s, order_t = iota((ROWS, ROWS), 0), iota((ROWS, ROWS), 1)
    seg_row = rows[SEG * HEADS : SEG * HEADS + 1, :]
    mask = jnp.where((order_t >= order_s) & (col(tab, SEG, 0) == seg_row), 0.0, MASKED)
    low = iota((ROWS, 2 * DIM), 1) < DIM
    grad_scores = jnp.zeros((ROWS, ROWS), F32)
    b_sum = jnp.zeros((ROWS, STATE), F32)
    c_sum = jnp.zeros((ROWS, STATE), F32)
    step_grad = jnp.zeros((HEADS, ROWS), F32)
    cum_grad = jnp.zeros((HEADS, ROWS), F32)
    state_dot = jnp.zeros((HEADS, ROWS), F32)
    tail_dot = jnp.zeros((HEADS, ROWS), F32)
    for j in range(PAIRS):
        x_pair = x[:, cols_of(j)].astype(F32)
        step = pair_cols(tab, STEP, j)
        scaled_f = x_pair * step
        scaled = scaled_f.astype(BF16)
        g = grad[:, cols_of(j)]
        g_f = g.astype(F32)
        zero = jnp.zeros_like(g)
        parts = []
        for k in range(2):
            h = 2 * j + k
            row = rows[CUM * HEADS + h : CUM * HEADS + h + 1, :]
            decay = jnp.exp(row - col(tab, CUM, h) + mask)
            own = jnp.where(low if k == 0 else jnp.logical_not(low), g, zero)
            grad_scores = grad_scores + nt(scaled, own) * decay
            parts.append(nn((decay * scores).astype(BF16), g))
        nxt = after[2 * j : 2 * j + 2].reshape(2 * DIM, STATE)
        prev = carried[2 * j : 2 * j + 2].reshape(2 * DIM, STATE)
        etail = pair_cols(tab, ETAIL, j)
        from_tail = etail * nt(b[...], nxt)
        total = jnp.where(low, parts[0], parts[1]) + from_tail
        gain = jnp.where(low, skip[2 * j], skip[2 * j + 1])
        grad_x[:, cols_of(j)] = (step * total + gain * g_f).astype(BF16)
        step_grad = step_grad + head_sums(j, x_pair * total)
        cum_grad = cum_grad + head_sums(j, g_f * inner[:, cols_of(j)])
        tail_dot = tail_dot + head_sums(j, scaled_f * from_tail)
        product = nxt.astype(F32) * prev.astype(F32)
        head = iota((HEADS, 2 * DIM), 0)
        own_rows = (head == 2 * j + iota((HEADS, 2 * DIM), 1) // DIM).astype(BF16)
        upper = product.astype(BF16)
        lower = (product - upper.astype(F32)).astype(BF16)
        state_dot = state_dot + nn(own_rows, upper) + nn(own_rows, lower)
        b_sum = b_sum + nn((etail * scaled_f).astype(BF16), nxt)
        c_sum = c_sum + nn((pair_cols(tab, ENTRY, j) * g_f).astype(BF16), prev)
    flow = grad_scores.astype(BF16)
    grad_b[...] = (b_sum + nn(flow, c[...])).astype(BF16)
    grad_c[...] = (c_sum + tn(flow, b[...])).astype(BF16)
    step_rows = rows[STEP * HEADS : (STEP + 1) * HEADS, :]
    through = rows[THROUGH * HEADS : (THROUGH + 1) * HEADS, :]
    end = jnp.sum(tail_dot, axis=1, keepdims=True) + jnp.sum(
        through * state_dot, axis=1, keepdims=True
    )
    cum_grad = cum_grad - step_rows * step_grad
    since = (iota((ROWS, ROWS), 0) >= iota((ROWS, ROWS), 1)).astype(F32)
    decay_grad = dot(cum_grad, since, ((1,), (0,)), HIGHEST) + end
    head = iota((HEADS, ROWS), 0)
    rate_rows = jnp.zeros((HEADS, ROWS), F32)
    for h in range(HEADS):
        rate_rows = jnp.where(head == h, rate[h], rate_rows)
    sig = rows[SIG * HEADS : (SIG + 1) * HEADS, :]
    grad_dt[...] = (step_grad - rate_rows * decay_grad) * sig


def backward(skip, rate, x, b, c, rows, tab, carried, inner, grad, after):
    outs = [
        ((ROWS, WIDE), BF16),
        ((HEADS, ROWS), F32),
        ((ROWS, STATE), BF16),
        ((ROWS, STATE), BF16),
    ]
    arrays = (x, b, c, rows, tab, carried, inner, grad, after)
    return staged(backward_kernel, (skip, rate), arrays, outs)


NEAR_FAR = (0, 1, 3, 2)


def project_kernel(
    place, grad, mixed, weight, rows, c, keep, send, grad_mix, out, ordered, acc
):
    at = pl.program_id(0)
    plane, core = place[0], place[1]
    planes, _, share, _ = mixed.shape

    @pl.when(at == 0)
    def _():
        acc[...] = jnp.zeros_like(acc)
        for k, step in enumerate(NEAR_FAR):
            to = (plane + step) % planes
            ordered[k * share : (k + 1) * share] = mixed[to, core]
            ordered[(planes + k) * share : (planes + k + 1) * share] = mixed[to, 1 - core]

    acc[...] += nt(weight[...], grad[...])
    both = nn(ordered[...], weight[...]).astype(BF16)
    keep[...] = both[: planes * share].reshape(keep.shape)
    send[...] = both[planes * share :].reshape(send.shape)

    @pl.when(at == pl.num_programs(0) - 1)
    def _():
        for h in range(HEADS):
            part = acc[h * DIM : (h + 1) * DIM].astype(BF16)
            entry = rows[ENTRY * HEADS + h : ENTRY * HEADS + h + 1, :]
            out[h] = nn((part.astype(F32) * entry).astype(BF16), c[...]).astype(BF16)
        for j in range(PAIRS):
            grad_mix[:, cols_of(j)] = acc[cols_of(j)].T.astype(BF16)


def project(place, grad, mixed, weight, rows, c):
    inner, width = weight.shape
    planes, sides, share, _ = mixed.shape
    tile = 1024
    fixed = lambda s: pl.BlockSpec(s, lambda i, r=len(s): (0,) * r)
    half = pl.BlockSpec((planes, share, tile), lambda i: (0, 0, i))
    tall = pl.BlockSpec((inner, tile), lambda i: (0, i))
    local = (HEADS, DIM, STATE)
    return pl.pallas_call(
        project_kernel,
        grid=(width // tile,),
        in_specs=smem(1)
        + [pl.BlockSpec((ROWS, tile), lambda i: (0, i)), fixed(mixed.shape), tall]
        + [fixed(rows.shape), fixed(c.shape)],
        out_specs=[half, half, fixed((ROWS, inner)), fixed(local)],
        out_shape=(
            jax.ShapeDtypeStruct((planes, share, width), BF16),
            jax.ShapeDtypeStruct((planes, share, width), BF16),
            jax.ShapeDtypeStruct((ROWS, inner), BF16),
            jax.ShapeDtypeStruct(local, BF16),
        ),
        scratch_shapes=[pltpu.VMEM((ROWS, inner), BF16), pltpu.VMEM((inner, ROWS), F32)],
        compiler_params=params(),
    )(place, grad, mixed, weight, rows, c)


def arrange_kernel(place, *refs):
    pieces, out, tokens, sems = refs[:10], refs[10], refs[11], refs[12]
    slabs, sides, share, cols = tokens.shape
    copies = []
    for side in range(2):
        core = place[1] if side == 0 else 1 - place[1]
        steps = (0, 3, 1, 2, 2)
        for k, piece in enumerate(pieces[side * 5 : side * 5 + 5]):
            at = 2 * ((place[0] + steps[k]) % 4) + core
            half = slabs // 2
            low, many = ((0, slabs), (0, slabs), (0, slabs), (0, half), (half, half))[k]
            target = tokens.at[low : low + many, at]
            copies.append(pltpu.make_async_copy(piece, target, sems.at[side * 5 + k]))
    for copy in copies:
        copy.start()
    for copy in copies:
        copy.wait()
    wide = sides * share
    for k in range(slabs):
        out[:, k * wide : (k + 1) * wide] = tokens[k].reshape(wide, cols).T


def arrange(place, pieces, slabs):
    share = 32
    cols = pieces[0].shape[1]
    views = [p.reshape(-1, share, cols) for p in pieces]
    return pl.pallas_call(
        arrange_kernel,
        in_specs=smem(1) + hbm(len(views)),
        out_specs=pl.BlockSpec(memory_space=pltpu.VMEM),
        out_shape=jax.ShapeDtypeStruct((cols, slabs * 8 * share), BF16),
        scratch_shapes=[
            pltpu.VMEM((slabs, 8, share, cols), BF16),
            pltpu.SemaphoreType.DMA((len(views),)),
        ],
        compiler_params=params(),
    )(place, *views)


def weight_kernel(left, right, out, acc):
    at = pl.program_id(0)

    @pl.when(at == 0)
    def _():
        acc[...] = nn(left[...], right[...])

    @pl.when(at > 0)
    def _():
        acc[...] += nn(left[...], right[...])

    @pl.when(at == pl.num_programs(0) - 1)
    def _():
        out[...] = acc[...].astype(BF16)


def weight_grad(left, right):
    cols, deep = left.shape
    wide = right.shape[1]
    tile = 512
    return pl.pallas_call(
        weight_kernel,
        grid=(deep // tile,),
        in_specs=[
            pl.BlockSpec((cols, tile), lambda i: (0, i)),
            pl.BlockSpec((tile, wide), lambda i: (i, 0)),
        ],
        out_specs=pl.BlockSpec((cols, wide), lambda i: (0, 0)),
        out_shape=jax.ShapeDtypeStruct((cols, wide), BF16),
        scratch_shapes=[pltpu.VMEM((cols, wide), F32)],
        compiler_params=params(),
    )(*pinned(left, right))


SWAP = [(i, i ^ 1) for i in range(8)]


def along_z(d):
    return [(2 * z + c, 2 * ((z + d) % 4) + c) for z in range(4) for c in range(2)]


def after(value, *others):
    return lax.optimization_barrier((value,) + others)[0]


def swap(value):
    return lax.ppermute(value, "tp", SWAP)


def up(value):
    return lax.ppermute(value, "tp", along_z(1))


def down(value):
    return lax.ppermute(value, "tp", along_z(-1))


def over_slabs(value):
    return lax.all_to_all(value, "ctx", 0, 0, tiled=True)


def shards(
    ssm_input,
    dt_raw,
    b_proj,
    c_proj,
    dt_bias,
    decay_rate,
    skip_gain,
    doc_start,
    out_weight,
    grad_out,
):
    share, width = grad_out.shape
    n_ctx = lax.axis_size("ctx")
    tp = lax.axis_index("tp").astype(jnp.int32)
    place = jnp.stack([tp // 2, tp % 2])
    b, c, x, dt, doc, weight = pinned(
        b_proj.reshape(ROWS, STATE),
        c_proj.reshape(ROWS, STATE),
        ssm_input,
        dt_raw.T,
        doc_start.reshape(1, ROWS),
        out_weight,
    )
    bias, rate, skip = pinned(dt_bias, decay_rate, skip_gain)

    grad_full = lax.all_gather(grad_out, "tp", axis=0, tiled=True)
    payload, rows, tab = states(bias, rate, x, dt, doc, b)
    carried, decay = prefix(over_slabs(payload))
    carried = over_slabs(carried)
    mixed, inner = mixer(skip, x, b, c, rows, tab, carried)
    (inner,) = pinned(inner)
    mixed_all = lax.all_gather(mixed, "ctx", axis=0, tiled=True)
    columns = lax.all_to_all(after(grad_out, decay), "ctx", 1, 0, tiled=True)

    keep, send, grad_mix, local = project(
        place, grad_full, mixed.reshape(4, 2, share, WIDE), weight, rows, c
    )
    local = over_slabs(local)
    taken = swap(send)
    half = share // 2
    columns = after(columns, keep)
    c_up, c_down = up(columns), down(columns)

    next_grad = over_slabs(suffix(local, decay))
    pair = keep.astype(F32) + taken.astype(F32)
    far_up, far_down = up(pair[3, :half].astype(BF16)), down(pair[3, half:].astype(BF16))
    split = columns.shape[0] // 2
    mine = (columns, c_up, c_down, up(c_up[:split]), down(c_down[split:]))
    pieces = mine + tuple(swap(piece) for piece in mine)
    top = jnp.concatenate([pair[1, :half] + far_up.astype(F32), pair[1, half:]], 0)
    low = jnp.concatenate([pair[2, :half], pair[2, half:] + far_down.astype(F32)], 0)
    from_low, from_top = up(top.astype(BF16)), down(low.astype(BF16))
    grad_x, grad_dt, grad_b, grad_c = backward(
        skip, rate, x, b, c, rows, tab, carried, inner, grad_mix, next_grad
    )
    layer_out = (pair[0] + from_low.astype(F32) + from_top.astype(F32)).astype(BF16)
    left = arrange(place, pieces, n_ctx)
    weight_sum = weight_grad(left, mixed_all)
    return (
        layer_out,
        grad_x,
        grad_dt.T,
        grad_b.reshape(ROWS, 1, STATE),
        grad_c.reshape(ROWS, 1, STATE),
        weight_sum,
    )


def solution(mesh):
    in_specs = (
        P("ctx", "tp"),
        P("ctx", "tp"),
        P("ctx", "tp", None),
        P("ctx", "tp", None),
        P("tp"),
        P("tp"),
        P("tp"),
        P("ctx"),
        P("tp", None),
        P(("ctx", "tp"), None),
    )
    out_specs = (
        P(("ctx", "tp"), None),
        P("ctx", "tp"),
        P("ctx", "tp"),
        P("ctx", "tp", None),
        P("ctx", "tp", None),
        P("ctx", "tp"),
    )
    return jax.shard_map(shards, mesh=mesh, in_specs=in_specs, out_specs=out_specs, check_vma=False)
```

```python
import jax
import jax.numpy as jnp
from jax import lax
from jax.experimental import pallas as pl
from jax.experimental.pallas import tpu as pltpu
from jax.sharding import PartitionSpec as P

F32 = jnp.float32
BF16 = jnp.bfloat16
HIGHEST = lax.Precision.HIGHEST
ROWS = 256
HEADS = 16
DIM = 64
STATE = 256
WIDE = HEADS * DIM
PAIRS = HEADS // 2
EXTRA = 8
MASKED = -1e30
CUM, STEP, ENTRY, ETAIL, TAIL, THROUGH, SEG, SIG = range(8)


def dot(a, b, dims, precision=None):
    return lax.dot_general(a, b, (dims, ((), ())), precision=precision, preferred_element_type=F32)


def nn(a, b):
    return dot(a, b, ((1,), (0,)))


def nt(a, b):
    return dot(a, b, ((1,), (1,)))


def tn(a, b):
    return dot(a, b, ((0,), (0,)))


def smem(n):
    return [pl.BlockSpec(memory_space=pltpu.SMEM)] * n


def hbm(n):
    return [pl.BlockSpec(memory_space=pltpu.HBM)] * n


def pinned(*arrays):
    return [pltpu.with_memory_space_constraint(a, pltpu.HBM) for a in arrays]


def staged(kernel, scalars, arrays, outs, us):
    given = list(scalars) + list(arrays)
    n, m = len(given), len(outs)

    def body(*refs):
        sources, results, local, sems = refs[:n], refs[n : n + m], refs[n + m : -1], refs[-1]
        copies = [
            pltpu.make_async_copy(a, b, sems.at[i])
            for i, (a, b) in enumerate(zip(sources, local[:n], strict=True))
        ]
        for copy in copies:
            copy.start()
        for copy in copies:
            copy.wait()
        kernel(*local)
        copies = [
            pltpu.make_async_copy(a, b, sems.at[n + i])
            for i, (a, b) in enumerate(zip(local[n:], results, strict=True))
        ]
        for copy in copies:
            copy.start()
        for copy in copies:
            copy.wait()

    return pl.pallas_call(
        body,
        in_specs=hbm(n),
        out_specs=hbm(m),
        out_shape=tuple(jax.ShapeDtypeStruct(*out) for out in outs),
        scratch_shapes=[pltpu.SMEM(a.shape, a.dtype) for a in scalars]
        + [pltpu.VMEM(a.shape, a.dtype) for a in arrays]
        + [pltpu.VMEM(*out) for out in outs]
        + [pltpu.SemaphoreType.DMA((n + m,))],
        compiler_params=params(),
        cost_estimate=took(us),
    )(*given)


def took(us):
    return pl.CostEstimate(flops=int(us * 1.1e9), bytes_accessed=0, transcendentals=0)


def params(mib=16):
    return pltpu.CompilerParams(vmem_limit_bytes=mib * 1024 * 1024)


def iota(shape, axis):
    return lax.broadcasted_iota(jnp.int32, shape, axis)


def col(tab, which, head):
    at = which * HEADS + head
    return tab[:, at : at + 1]


def pair_cols(tab, which, pair):
    low = iota((ROWS, 2 * DIM), 1) < DIM
    return jnp.where(low, col(tab, which, 2 * pair), col(tab, which, 2 * pair + 1))


def cols_of(pair):
    return slice(pair * 2 * DIM, (pair + 1) * 2 * DIM)


def states_kernel(bias, rate, x, dt, doc, b, payload, tab_rows, tab_cols):
    head = iota((HEADS, ROWS), 0)
    bias_rows = jnp.zeros((HEADS, ROWS), F32)
    rate_rows = jnp.zeros((HEADS, ROWS), F32)
    for h in range(HEADS):
        bias_rows = jnp.where(head == h, bias[h], bias_rows)
        rate_rows = jnp.where(head == h, rate[h], rate_rows)
    raw = dt[...] + bias_rows
    small = jnp.exp(-jnp.abs(raw))
    step = jnp.maximum(raw, 0.0) + jnp.log1p(small)
    sig = jnp.where(raw >= 0, 1.0, small) / (1.0 + small)
    upto = (iota((ROWS, ROWS), 0) <= iota((ROWS, ROWS), 1)).astype(F32)
    cum = dot(-step * rate_rows, upto, ((1,), (0,)), HIGHEST)
    starts = jnp.broadcast_to(doc[...].astype(F32), (HEADS, ROWS))
    seg = nn(starts.astype(BF16), upto.astype(BF16))
    last = cum[:, ROWS - 1 :]
    seg_last = seg[:, ROWS - 1 :]
    entry = jnp.where(seg == 0.0, jnp.exp(cum), 0.0)
    etail = jnp.where(seg == seg_last, jnp.exp(last - cum), 0.0)
    through = jnp.broadcast_to(jnp.where(seg_last == 0.0, jnp.exp(last), 0.0), (HEADS, ROWS))
    rows = jnp.concatenate([cum, step, entry, etail, etail * step, through, seg, sig], axis=0)
    tab_rows[...] = rows
    tab = rows.T
    tab_cols[...] = tab
    for j in range(PAIRS):
        weighted = (x[:, cols_of(j)].astype(F32) * pair_cols(tab, TAIL, j)).astype(BF16)
        state = tn(weighted, b[...]).astype(BF16)
        payload[2 * j, :DIM, :] = state[:DIM]
        payload[2 * j + 1, :DIM, :] = state[DIM:]
    upper = through.astype(BF16).astype(F32)
    lower = through - upper
    which = iota((EXTRA, ROWS), 0)
    for h in range(HEADS):
        tail_rows = jnp.where(which == 0, upper[h : h + 1], jnp.where(which == 1, lower[h : h + 1], 0.0))
        payload[h, DIM:, :] = tail_rows.astype(BF16)


def states(bias, rate, x, dt, doc, b):
    outs = [
        ((HEADS, DIM + EXTRA, STATE), BF16),
        ((8 * HEADS, ROWS), F32),
        ((ROWS, 8 * HEADS), F32),
    ]
    return staged(states_kernel, (bias, rate), (x, dt, doc, b), outs, 3.3)


def prefix_kernel(got, out, decay):
    slabs = got.shape[0]
    carry = jnp.zeros((DIM, STATE), F32)
    for c in range(slabs):
        out[c] = carry.astype(BF16)
        extra = got[c, DIM:, :].astype(F32)
        through = extra[0:1] + extra[1:2]
        decay[c : c + 1, :] = through
        carry = through * carry + got[c, :DIM, :].astype(F32)


def prefix(got):
    slabs = got.shape[0]
    outs = [((slabs, DIM, STATE), BF16), ((slabs, STATE), F32)]
    return staged(prefix_kernel, (), (got,), outs, 0.5)


def suffix_kernel(got, decay, out):
    slabs = got.shape[0]
    carry = jnp.zeros((DIM, STATE), F32)
    for c in reversed(range(slabs)):
        out[c] = carry.astype(BF16)
        carry = decay[c : c + 1, :] * carry + got[c].astype(F32)


def suffix(got, decay):
    return staged(suffix_kernel, (), (got, decay), [(got.shape, BF16)], 1.2)[0]


def mixer_kernel(skip, x, b, c, rows, tab_ref, carried, mixed, inner):
    tab = tab_ref[...]
    scores = nt(c[...], b[...])
    order_t, order_s = iota((ROWS, ROWS), 0), iota((ROWS, ROWS), 1)
    seg_row = rows[SEG * HEADS : SEG * HEADS + 1, :]
    mask = jnp.where((order_t >= order_s) & (col(tab, SEG, 0) == seg_row), 0.0, MASKED)
    low = iota((ROWS, 2 * DIM), 1) < DIM
    for j in range(PAIRS):
        x_pair = x[:, cols_of(j)].astype(F32)
        scaled = (x_pair * pair_cols(tab, STEP, j)).astype(BF16)
        parts = []
        for h in (2 * j, 2 * j + 1):
            row = rows[CUM * HEADS + h : CUM * HEADS + h + 1, :]
            weight = jnp.exp(col(tab, CUM, h) - row + mask) * scores
            parts.append(nn(weight.astype(BF16), scaled))
        state = carried[2 * j : 2 * j + 2].reshape(2 * DIM, STATE)
        got = jnp.where(low, parts[0], parts[1]) + pair_cols(tab, ENTRY, j) * nt(c[...], state)
        inner[:, cols_of(j)] = got
        gain = jnp.where(low, skip[2 * j], skip[2 * j + 1])
        mixed[:, cols_of(j)] = (got + gain * x_pair).astype(BF16)


def mixer(skip, x, b, c, rows, tab, carried):
    outs = [((ROWS, WIDE), BF16), ((ROWS, WIDE), F32)]
    return staged(mixer_kernel, (skip,), (x, b, c, rows, tab, carried), outs, 4.2)


def head_sums(pair, values):
    head = iota((HEADS, 2 * DIM), 0)
    own = (head == 2 * pair + iota((HEADS, 2 * DIM), 1) // DIM).astype(BF16)
    upper = values.astype(BF16)
    lower = (values - upper.astype(F32)).astype(BF16)
    return nt(own, upper) + nt(own, lower)


def inside_kernel(x, b, c, rows, tab_ref, carried, inner, grad, part, grad_c, b_part, cum_part):
    tab = tab_ref[...]
    scores = nt(b[...], c[...])
    order_s, order_t = iota((ROWS, ROWS), 0), iota((ROWS, ROWS), 1)
    seg_row = rows[SEG * HEADS : SEG * HEADS + 1, :]
    mask = jnp.where((order_t >= order_s) & (col(tab, SEG, 0) == seg_row), 0.0, MASKED)
    low = iota((ROWS, 2 * DIM), 1) < DIM
    grad_scores = jnp.zeros((ROWS, ROWS), F32)
    c_sum = jnp.zeros((ROWS, STATE), F32)
    cum_grad = jnp.zeros((HEADS, ROWS), F32)
    for j in range(PAIRS):
        scaled = (x[:, cols_of(j)].astype(F32) * pair_cols(tab, STEP, j)).astype(BF16)
        g = grad[:, cols_of(j)]
        g_f = g.astype(F32)
        zero = jnp.zeros_like(g)
        parts = []
        for k in range(2):
            h = 2 * j + k
            row = rows[CUM * HEADS + h : CUM * HEADS + h + 1, :]
            decay = jnp.exp(row - col(tab, CUM, h) + mask)
            own = jnp.where(low if k == 0 else jnp.logical_not(low), g, zero)
            grad_scores = grad_scores + nt(scaled, own) * decay
            parts.append(nn((decay * scores).astype(BF16), g))
        part[:, cols_of(j)] = jnp.where(low, parts[0], parts[1])
        prev = carried[2 * j : 2 * j + 2].reshape(2 * DIM, STATE)
        cum_grad = cum_grad + head_sums(j, g_f * inner[:, cols_of(j)])
        c_sum = c_sum + nn((pair_cols(tab, ENTRY, j) * g_f).astype(BF16), prev)
    flow = grad_scores.astype(BF16)
    b_part[...] = nn(flow, c[...])
    grad_c[...] = (c_sum + tn(flow, b[...])).astype(BF16)
    cum_part[...] = cum_grad


def inside_grads(x, b, c, rows, tab, carried, inner, grad):
    outs = [
        ((ROWS, WIDE), F32),
        ((ROWS, STATE), BF16),
        ((ROWS, STATE), F32),
        ((HEADS, ROWS), F32),
    ]
    return staged(inside_kernel, (), (x, b, c, rows, tab, carried, inner, grad), outs, 5.0)


def backward_kernel(
    skip, rate, x, b, rows, tab_ref, carried, grad, part, b_part, cum_part, after, grad_x, grad_dt, grad_b
):
    tab = tab_ref[...]
    low = iota((ROWS, 2 * DIM), 1) < DIM
    b_sum = b_part[...]
    step_grad = jnp.zeros((HEADS, ROWS), F32)
    state_dot = jnp.zeros((HEADS, ROWS), F32)
    tail_dot = jnp.zeros((HEADS, ROWS), F32)
    for j in range(PAIRS):
        x_pair = x[:, cols_of(j)].astype(F32)
        step = pair_cols(tab, STEP, j)
        scaled = x_pair * step
        g_f = grad[:, cols_of(j)].astype(F32)
        nxt = after[2 * j : 2 * j + 2].reshape(2 * DIM, STATE)
        prev = carried[2 * j : 2 * j + 2].reshape(2 * DIM, STATE)
        etail = pair_cols(tab, ETAIL, j)
        from_tail = etail * nt(b[...], nxt)
        total = part[:, cols_of(j)] + from_tail
        gain = jnp.where(low, skip[2 * j], skip[2 * j + 1])
        grad_x[:, cols_of(j)] = (step * total + gain * g_f).astype(BF16)
        step_grad = step_grad + head_sums(j, x_pair * total)
        tail_dot = tail_dot + head_sums(j, scaled * from_tail)
        product = nxt.astype(F32) * prev.astype(F32)
        head = iota((HEADS, 2 * DIM), 0)
        own_rows = (head == 2 * j + iota((HEADS, 2 * DIM), 1) // DIM).astype(BF16)
        upper = product.astype(BF16)
        lower = (product - upper.astype(F32)).astype(BF16)
        state_dot = state_dot + nn(own_rows, upper) + nn(own_rows, lower)
        b_sum = b_sum + nn((etail * scaled).astype(BF16), nxt)
    grad_b[...] = b_sum.astype(BF16)
    step_rows = rows[STEP * HEADS : (STEP + 1) * HEADS, :]
    through = rows[THROUGH * HEADS : (THROUGH + 1) * HEADS, :]
    end = jnp.sum(tail_dot, axis=1, keepdims=True) + jnp.sum(
        through * state_dot, axis=1, keepdims=True
    )
    cum_grad = cum_part[...] - step_rows * step_grad
    since = (iota((ROWS, ROWS), 0) >= iota((ROWS, ROWS), 1)).astype(F32)
    decay_grad = dot(cum_grad, since, ((1,), (0,)), HIGHEST) + end
    head = iota((HEADS, ROWS), 0)
    rate_rows = jnp.zeros((HEADS, ROWS), F32)
    for h in range(HEADS):
        rate_rows = jnp.where(head == h, rate[h], rate_rows)
    sig = rows[SIG * HEADS : (SIG + 1) * HEADS, :]
    grad_dt[...] = (step_grad - rate_rows * decay_grad) * sig


def backward(skip, rate, x, b, rows, tab, carried, grad, part, b_part, cum_part, after):
    outs = [((ROWS, WIDE), BF16), ((HEADS, ROWS), F32), ((ROWS, STATE), BF16)]
    arrays = (x, b, rows, tab, carried, grad, part, b_part, cum_part, after)
    return staged(backward_kernel, (skip, rate), arrays, outs, 5.0)


NEAR_FAR = (0, 1, 3, 2)
CHUNKS = 8


def start(*copies):
    for copy in copies:
        copy.start()


def wait(*copies):
    for copy in copies:
        copy.wait()


def paced(loads, ahead=2):
    for batch in loads[:ahead]:
        start(*batch)
    for n, batch in enumerate(loads):
        wait(*batch)
        if n + ahead < len(loads):
            start(*loads[n + ahead])
        yield n


def vmem(n):
    return [pl.BlockSpec(memory_space=pltpu.VMEM)] * n


def project_kernel(
    place, grad_hbm, weight_hbm, mixed, rows, c, keep, send, grad_mix, out, *scratch
):
    grad, weight, ordered, acc, sems = scratch
    plane, core = place[0], place[1]
    planes, _, share, _ = mixed.shape
    tile = weight.shape[1] // CHUNKS
    loads = []
    for n in range(CHUNKS):
        cols = pl.ds(n * tile, tile)
        loads.append(
            (
                pltpu.make_async_copy(grad_hbm.at[:, cols], grad.at[:, cols], sems.at[0, n]),
                pltpu.make_async_copy(weight_hbm.at[:, cols], weight.at[:, cols], sems.at[1, n]),
            )
        )
    for n in paced(loads):
        if n == 0:
            for k, step in enumerate(NEAR_FAR):
                to = (plane + step) % planes
                ordered[k * share : (k + 1) * share] = mixed[to, core]
                ordered[(planes + k) * share : (planes + k + 1) * share] = mixed[to, 1 - core]
        cols = slice(n * tile, (n + 1) * tile)
        part = nt(weight[:, cols], grad[:, cols])
        if n == 0:
            acc[...] = part
        else:
            acc[...] += part
        both = nn(ordered[...], weight[:, cols]).astype(BF16)
        keep[:, :, cols] = both[: planes * share].reshape(planes, share, tile)
        send[:, :, cols] = both[planes * share :].reshape(planes, share, tile)
    for h in range(HEADS):
        part = acc[h * DIM : (h + 1) * DIM].astype(BF16)
        entry = rows[ENTRY * HEADS + h : ENTRY * HEADS + h + 1, :]
        out[h] = nn((part.astype(F32) * entry).astype(BF16), c[...]).astype(BF16)
    for j in range(PAIRS):
        grad_mix[:, cols_of(j)] = acc[cols_of(j)].T.astype(BF16)


def project(place, grad, weight, mixed, rows, c):
    inner, width = weight.shape
    planes, _, share, _ = mixed.shape
    return pl.pallas_call(
        project_kernel,
        in_specs=smem(1) + hbm(2) + vmem(3),
        out_specs=vmem(4),
        out_shape=(
            jax.ShapeDtypeStruct((planes, share, width), BF16),
            jax.ShapeDtypeStruct((planes, share, width), BF16),
            jax.ShapeDtypeStruct((ROWS, inner), BF16),
            jax.ShapeDtypeStruct((HEADS, DIM, STATE), BF16),
        ),
        scratch_shapes=[
            pltpu.VMEM(grad.shape, BF16),
            pltpu.VMEM(weight.shape, BF16),
            pltpu.VMEM((ROWS, inner), BF16),
            pltpu.VMEM((inner, ROWS), F32),
            pltpu.SemaphoreType.DMA((2, CHUNKS)),
        ],
        compiler_params=params(36),
        cost_estimate=took(10.0),
    )(place, *pinned(grad), weight, mixed, rows, c)


def plane_sums(keep, taken, first, rest, outs, combine):
    n = len(first)
    shape = keep.shape[1:]

    def body(*refs):
        a_hbm, b_hbm = refs[:2]
        extra = refs[2 : 2 + len(rest)]
        results = refs[2 + len(rest) : 2 + len(rest) + len(outs)]
        a, b = refs[-3 - len(rest) : -1 - len(rest)]
        local, sems = refs[-1 - len(rest) : -1], refs[-1]
        copies = [
            pltpu.make_async_copy(source, target, sems.at[k])
            for k, (source, target) in enumerate(zip(extra, local, strict=True))
        ]
        for k, plane in enumerate(first):
            for side, (source, target) in enumerate(((a_hbm, a), (b_hbm, b))):
                at = len(rest) + 2 * k + side
                copies.append(pltpu.make_async_copy(source.at[plane], target.at[k], sems.at[at]))
        start(*copies)
        wait(*copies)
        combine(a, b, local, results)

    return pl.pallas_call(
        body,
        in_specs=hbm(2 + len(rest)),
        out_specs=vmem(len(outs)),
        out_shape=tuple(jax.ShapeDtypeStruct(out, BF16) for out in outs),
        scratch_shapes=[pltpu.VMEM((n,) + shape, BF16)] * 2
        + [pltpu.VMEM(r.shape, BF16) for r in rest]
        + [pltpu.SemaphoreType.DMA((len(rest) + 2 * n,))],
        compiler_params=params(),
        cost_estimate=took(1.5),
    )(keep, taken, *rest)


def add(*parts):
    total = parts[0].astype(F32)
    for part in parts[1:]:
        total = total + part.astype(F32)
    return total


def far_sums(a, b, rest, results):
    half = a.shape[1] // 2
    for k in range(2):
        rows = slice(k * half, (k + 1) * half)
        results[k][...] = add(a[0, rows], b[0, rows]).astype(BF16)


def near_sums(a, b, rest, results):
    half = a.shape[1] // 2
    for k in range(2):
        for part in range(2):
            rows = slice(part * half, (part + 1) * half)
            extra = (rest[k][...],) if part == k else ()
            results[k][rows] = add(a[k, rows], b[k, rows], *extra).astype(BF16)


def last_sum(a, b, rest, results):
    results[0][...] = add(a[0], b[0], rest[0][...], rest[1][...]).astype(BF16)


def arrange_kernel(place, *refs):
    pieces, result, tokens, out, sems = refs[:8], refs[8], refs[9], refs[10], refs[11]
    slabs, sides, share, cols = tokens.shape
    copies = []
    for side in range(2):
        core = place[1] if side == 0 else 1 - place[1]
        for k, piece in enumerate(pieces[side * 4 : side * 4 + 4]):
            at = 2 * ((place[0] + (0, 3, 1, 2)[k]) % 4) + core
            copies.append(pltpu.make_async_copy(piece, tokens.at[:, at], sems.at[side * 4 + k]))
    for copy in copies:
        copy.start()
    for copy in copies:
        copy.wait()
    wide = sides * share
    stores = []
    for k in range(slabs):
        out[:, k * wide : (k + 1) * wide] = tokens[k].reshape(wide, cols).T
        if k % 4 == 3:
            done = pl.ds((k - 3) * wide, 4 * wide)
            stores.append(
                pltpu.make_async_copy(out.at[:, done], result.at[:, done], sems.at[8 + k // 4])
            )
            start(stores[-1])
    wait(*stores)


def arrange(place, pieces, slabs):
    share = 32
    cols = pieces[0].shape[1]
    views = [p.reshape(-1, share, cols) for p in pieces]
    return pl.pallas_call(
        arrange_kernel,
        in_specs=smem(1) + hbm(len(views)),
        out_specs=hbm(1)[0],
        out_shape=jax.ShapeDtypeStruct((cols, slabs * 8 * share), BF16),
        scratch_shapes=[
            pltpu.VMEM((slabs, 8, share, cols), BF16),
            pltpu.VMEM((cols, slabs * 8 * share), BF16),
            pltpu.SemaphoreType.DMA((len(views) + slabs // 4,)),
        ],
        compiler_params=params(),
        cost_estimate=took(3.5),
    )(place, *views)


def weight_kernel(left_hbm, right_hbm, out, left, right, acc, sems):
    steps = sems.shape[1]
    tile = left.shape[1] // steps
    spans = [pl.ds(n * tile, tile) for n in range(steps)]
    loads = [
        (
            pltpu.make_async_copy(left_hbm.at[:, span], left.at[:, span], sems.at[0, n]),
            pltpu.make_async_copy(right_hbm.at[span], right.at[span], sems.at[1, n]),
        )
        for n, span in enumerate(spans)
    ]
    for n in paced(loads):
        span = slice(n * tile, (n + 1) * tile)
        part = nn(left[:, span], right[span])
        if n == 0:
            acc[...] = part
        elif n < steps - 1:
            acc[...] += part
        else:
            out[...] = (acc[...] + part).astype(BF16)


def weight_grad(left, right):
    cols, _ = left.shape
    wide = right.shape[1]
    return pl.pallas_call(
        weight_kernel,
        in_specs=hbm(2),
        out_specs=vmem(1)[0],
        out_shape=jax.ShapeDtypeStruct((cols, wide), BF16),
        scratch_shapes=[
            pltpu.VMEM(left.shape, BF16),
            pltpu.VMEM(right.shape, BF16),
            pltpu.VMEM((cols, wide), F32),
            pltpu.SemaphoreType.DMA((2, 4)),
        ],
        compiler_params=params(22),
        cost_estimate=took(7.0),
    )(*pinned(left, right))


SWAP = [(i, i ^ 1) for i in range(8)]


def along_z(d):
    return [(2 * z + c, 2 * ((z + d) % 4) + c) for z in range(4) for c in range(2)]


def after(value, *others):
    return lax.optimization_barrier((value,) + others)[0]


def swap(value):
    return lax.ppermute(value, "tp", SWAP)


def up(value):
    return lax.ppermute(value, "tp", along_z(1))


def down(value):
    return lax.ppermute(value, "tp", along_z(-1))


def over_slabs(value):
    return lax.all_to_all(value, "ctx", 0, 0, tiled=True)


def shards(
    ssm_input,
    dt_raw,
    b_proj,
    c_proj,
    dt_bias,
    decay_rate,
    skip_gain,
    doc_start,
    out_weight,
    grad_out,
):
    share, width = grad_out.shape
    n_ctx = lax.axis_size("ctx")
    tp = lax.axis_index("tp").astype(jnp.int32)
    place = jnp.stack([tp // 2, tp % 2])
    b, c, x, dt, doc, weight = pinned(
        b_proj.reshape(ROWS, STATE),
        c_proj.reshape(ROWS, STATE),
        ssm_input,
        dt_raw.T,
        doc_start.reshape(1, ROWS),
        out_weight,
    )
    bias, rate, skip = pinned(dt_bias, decay_rate, skip_gain)

    grad_full = lax.all_gather(grad_out, "tp", axis=0, tiled=True)
    payload, rows, tab = states(bias, rate, x, dt, doc, b)
    rows, tab = pinned(rows, tab)
    carried, decay = prefix(over_slabs(payload))
    (carried,) = pinned(over_slabs(carried))
    mixed, inner = mixer(skip, x, b, c, rows, tab, carried)
    (inner,) = pinned(inner)
    mixed_all = lax.all_gather(mixed, "ctx", axis=0, tiled=True)
    columns = lax.all_to_all(after(grad_out, decay), "ctx", 1, 0, tiled=True)

    keep, send, grad_mix, local = project(
        place, grad_full, weight, mixed.reshape(4, 2, share, WIDE), rows, c
    )
    local, columns, send = lax.optimization_barrier((local, columns, send))
    c_up, c_down = up(columns), down(columns)
    local = over_slabs(local)
    taken = swap(send)
    half = share // 2
    keep, grad_mix = pinned(keep, grad_mix)
    far = plane_sums(keep, taken, (3,), (), ((half, width),) * 2, far_sums)
    far = up(far[0]), down(far[1])
    c_far = up(c_up)
    next_grad = suffix(local, decay)
    next_grad, taken, grad_mix, c_down = lax.optimization_barrier(
        (next_grad, taken, grad_mix, c_down)
    )
    next_grad = over_slabs(next_grad)
    grads = inside_grads(x, b, c, rows, tab, carried, inner, grad_mix)
    grad_c = grads[1]
    part, b_part, cum_part = pinned(grads[0], grads[2], grads[3])
    near = plane_sums(keep, taken, (1, 2), far, ((share, width),) * 2, near_sums)
    near = up(near[0]), down(near[1])
    mine = (columns, c_up, c_down, c_far)
    pieces = mine + tuple(swap(piece) for piece in mine)
    left = arrange(place, pieces, n_ctx)
    next_grad, left = lax.optimization_barrier((next_grad, left))
    grad_x, grad_dt, grad_b = backward(
        skip, rate, x, b, rows, tab, carried, grad_mix, part, b_part, cum_part, next_grad
    )
    (layer_out,) = plane_sums(keep, taken, (0,), near, ((share, width),), last_sum)
    weight_sum = weight_grad(left, after(mixed_all, layer_out))
    return (
        layer_out,
        grad_x,
        grad_dt.T,
        grad_b.reshape(ROWS, 1, STATE),
        grad_c.reshape(ROWS, 1, STATE),
        weight_sum,
    )


def solution(mesh):
    in_specs = (
        P("ctx", "tp"),
        P("ctx", "tp"),
        P("ctx", "tp", None),
        P("ctx", "tp", None),
        P("tp"),
        P("tp"),
        P("tp"),
        P("ctx"),
        P("tp", None),
        P(("ctx", "tp"), None),
    )
    out_specs = (
        P(("ctx", "tp"), None),
        P("ctx", "tp"),
        P("ctx", "tp"),
        P("ctx", "tp", None),
        P("ctx", "tp", None),
        P("ctx", "tp"),
    )
    return jax.shard_map(shards, mesh=mesh, in_specs=in_specs, out_specs=out_specs, check_vma=False)
```

```python
import jax
import jax.numpy as jnp
from jax import lax
from jax.experimental import pallas as pl
from jax.experimental.pallas import tpu as pltpu
from jax.sharding import PartitionSpec as P

F32 = jnp.float32
BF16 = jnp.bfloat16
HIGHEST = lax.Precision.HIGHEST
ROWS = 256
HEADS = 16
DIM = 64
STATE = 256
WIDE = HEADS * DIM
PAIRS = HEADS // 2
EXTRA = 8
MASKED = -1e30
CUM, STEP, ENTRY, ETAIL, TAIL, THROUGH, SEG, SIG = range(8)


def dot(a, b, dims, precision=None):
    return lax.dot_general(a, b, (dims, ((), ())), precision=precision, preferred_element_type=F32)


def nn(a, b):
    return dot(a, b, ((1,), (0,)))


def nt(a, b):
    return dot(a, b, ((1,), (1,)))


def tn(a, b):
    return dot(a, b, ((0,), (0,)))


def smem(n):
    return [pl.BlockSpec(memory_space=pltpu.SMEM)] * n


def hbm(n):
    return [pl.BlockSpec(memory_space=pltpu.HBM)] * n


def pinned(*arrays):
    return [pltpu.with_memory_space_constraint(a, pltpu.HBM) for a in arrays]


def staged(kernel, scalars, arrays, outs, us, mib=16):
    given = list(scalars) + list(arrays)
    n, m = len(given), len(outs)

    def body(*refs):
        sources, results, local, sems = refs[:n], refs[n : n + m], refs[n + m : -1], refs[-1]
        copies = [
            pltpu.make_async_copy(a, b, sems.at[i])
            for i, (a, b) in enumerate(zip(sources, local[:n], strict=True))
        ]
        for copy in copies:
            copy.start()
        for copy in copies:
            copy.wait()
        kernel(*local)
        copies = [
            pltpu.make_async_copy(a, b, sems.at[n + i])
            for i, (a, b) in enumerate(zip(local[n:], results, strict=True))
        ]
        for copy in copies:
            copy.start()
        for copy in copies:
            copy.wait()

    return pl.pallas_call(
        body,
        in_specs=hbm(n),
        out_specs=hbm(m),
        out_shape=tuple(jax.ShapeDtypeStruct(*out) for out in outs),
        scratch_shapes=[pltpu.SMEM(a.shape, a.dtype) for a in scalars]
        + [pltpu.VMEM(a.shape, a.dtype) for a in arrays]
        + [pltpu.VMEM(*out) for out in outs]
        + [pltpu.SemaphoreType.DMA((n + m,))],
        compiler_params=params(mib),
        cost_estimate=took(us),
    )(*given)


def took(us):
    return pl.CostEstimate(flops=int(us * 1.1e9), bytes_accessed=0, transcendentals=0)


def params(mib=16):
    return pltpu.CompilerParams(vmem_limit_bytes=mib * 1024 * 1024)


def iota(shape, axis):
    return lax.broadcasted_iota(jnp.int32, shape, axis)


def col(tab, which, head):
    at = which * HEADS + head
    return tab[:, at : at + 1]


def pair_cols(tab, which, pair):
    low = iota((ROWS, 2 * DIM), 1) < DIM
    return jnp.where(low, col(tab, which, 2 * pair), col(tab, which, 2 * pair + 1))


def cols_of(pair):
    return slice(pair * 2 * DIM, (pair + 1) * 2 * DIM)


def states_kernel(bias, rate, x, dt, doc, b, payload, tab_rows, tab_cols):
    head = iota((HEADS, ROWS), 0)
    bias_rows = jnp.zeros((HEADS, ROWS), F32)
    rate_rows = jnp.zeros((HEADS, ROWS), F32)
    for h in range(HEADS):
        bias_rows = jnp.where(head == h, bias[h], bias_rows)
        rate_rows = jnp.where(head == h, rate[h], rate_rows)
    raw = dt[...] + bias_rows
    small = jnp.exp(-jnp.abs(raw))
    step = jnp.maximum(raw, 0.0) + jnp.log1p(small)
    sig = jnp.where(raw >= 0, 1.0, small) / (1.0 + small)
    upto = (iota((ROWS, ROWS), 0) <= iota((ROWS, ROWS), 1)).astype(F32)
    cum = dot(-step * rate_rows, upto, ((1,), (0,)), HIGHEST)
    starts = jnp.broadcast_to(doc[...].astype(F32), (HEADS, ROWS))
    seg = nn(starts.astype(BF16), upto.astype(BF16))
    last = cum[:, ROWS - 1 :]
    seg_last = seg[:, ROWS - 1 :]
    entry = jnp.where(seg == 0.0, jnp.exp(cum), 0.0)
    etail = jnp.where(seg == seg_last, jnp.exp(last - cum), 0.0)
    through = jnp.broadcast_to(jnp.where(seg_last == 0.0, jnp.exp(last), 0.0), (HEADS, ROWS))
    rows = jnp.concatenate([cum, step, entry, etail, etail * step, through, seg, sig], axis=0)
    tab_rows[...] = rows
    tab = rows.T
    tab_cols[...] = tab
    for j in range(PAIRS):
        weighted = (x[:, cols_of(j)].astype(F32) * pair_cols(tab, TAIL, j)).astype(BF16)
        state = tn(weighted, b[...]).astype(BF16)
        payload[2 * j, :DIM, :] = state[:DIM]
        payload[2 * j + 1, :DIM, :] = state[DIM:]
    upper = through.astype(BF16).astype(F32)
    lower = through - upper
    which = iota((EXTRA, ROWS), 0)
    for h in range(HEADS):
        tail_rows = jnp.where(which == 0, upper[h : h + 1], jnp.where(which == 1, lower[h : h + 1], 0.0))
        payload[h, DIM:, :] = tail_rows.astype(BF16)


def states(bias, rate, x, dt, doc, b):
    outs = [
        ((HEADS, DIM + EXTRA, STATE), BF16),
        ((8 * HEADS, ROWS), F32),
        ((ROWS, 8 * HEADS), F32),
    ]
    return staged(states_kernel, (bias, rate), (x, dt, doc, b), outs, 3.3)


def prefix_kernel(got, out, decay):
    slabs = got.shape[0]
    carry = jnp.zeros((DIM, STATE), F32)
    for c in range(slabs):
        out[c] = carry.astype(BF16)
        extra = got[c, DIM:, :].astype(F32)
        through = extra[0:1] + extra[1:2]
        decay[c : c + 1, :] = through
        carry = through * carry + got[c, :DIM, :].astype(F32)


def prefix(got):
    slabs = got.shape[0]
    outs = [((slabs, DIM, STATE), BF16), ((slabs, STATE), F32)]
    return staged(prefix_kernel, (), (got,), outs, 0.5)


def suffix_kernel(got, decay, out):
    slabs = got.shape[0]
    carry = jnp.zeros((DIM, STATE), F32)
    for c in reversed(range(slabs)):
        out[c] = carry.astype(BF16)
        carry = decay[c : c + 1, :] * carry + got[c].astype(F32)


def suffix(got, decay):
    return staged(suffix_kernel, (), (got, decay), [(got.shape, BF16)], 1.2)[0]


def mixer_kernel(skip, x, b, c, rows, tab_ref, carried, mixed, inner):
    tab = tab_ref[...]
    scores = nt(c[...], b[...])
    order_t, order_s = iota((ROWS, ROWS), 0), iota((ROWS, ROWS), 1)
    seg_row = rows[SEG * HEADS : SEG * HEADS + 1, :]
    mask = jnp.where((order_t >= order_s) & (col(tab, SEG, 0) == seg_row), 0.0, MASKED)
    low = iota((ROWS, 2 * DIM), 1) < DIM
    for j in range(PAIRS):
        x_pair = x[:, cols_of(j)].astype(F32)
        scaled = (x_pair * pair_cols(tab, STEP, j)).astype(BF16)
        parts = []
        for h in (2 * j, 2 * j + 1):
            row = rows[CUM * HEADS + h : CUM * HEADS + h + 1, :]
            weight = jnp.exp(col(tab, CUM, h) - row + mask) * scores
            parts.append(nn(weight.astype(BF16), scaled))
        state = carried[2 * j : 2 * j + 2].reshape(2 * DIM, STATE)
        got = jnp.where(low, parts[0], parts[1]) + pair_cols(tab, ENTRY, j) * nt(c[...], state)
        inner[:, cols_of(j)] = got
        gain = jnp.where(low, skip[2 * j], skip[2 * j + 1])
        mixed[:, cols_of(j)] = (got + gain * x_pair).astype(BF16)


def mixer(skip, x, b, c, rows, tab, carried):
    outs = [((ROWS, WIDE), BF16), ((ROWS, WIDE), F32)]
    return staged(mixer_kernel, (skip,), (x, b, c, rows, tab, carried), outs, 4.2, 60)


def head_sums(pair, values):
    head = iota((HEADS, 2 * DIM), 0)
    own = (head == 2 * pair + iota((HEADS, 2 * DIM), 1) // DIM).astype(BF16)
    upper = values.astype(BF16)
    lower = (values - upper.astype(F32)).astype(BF16)
    return nt(own, upper) + nt(own, lower)


def inside_kernel(x, b, c, rows, tab_ref, carried, inner, grad, part, grad_c, b_part, cum_part):
    tab = tab_ref[...]
    scores = nt(b[...], c[...])
    order_s, order_t = iota((ROWS, ROWS), 0), iota((ROWS, ROWS), 1)
    seg_row = rows[SEG * HEADS : SEG * HEADS + 1, :]
    mask = jnp.where((order_t >= order_s) & (col(tab, SEG, 0) == seg_row), 0.0, MASKED)
    low = iota((ROWS, 2 * DIM), 1) < DIM
    grad_scores = jnp.zeros((ROWS, ROWS), F32)
    c_sum = jnp.zeros((ROWS, STATE), F32)
    cum_grad = jnp.zeros((HEADS, ROWS), F32)
    for j in range(PAIRS):
        scaled = (x[:, cols_of(j)].astype(F32) * pair_cols(tab, STEP, j)).astype(BF16)
        g = grad[:, cols_of(j)]
        g_f = g.astype(F32)
        zero = jnp.zeros_like(g)
        parts = []
        for k in range(2):
            h = 2 * j + k
            row = rows[CUM * HEADS + h : CUM * HEADS + h + 1, :]
            decay = jnp.exp(row - col(tab, CUM, h) + mask)
            own = jnp.where(low if k == 0 else jnp.logical_not(low), g, zero)
            grad_scores = grad_scores + nt(scaled, own) * decay
            parts.append(nn((decay * scores).astype(BF16), g))
        part[:, cols_of(j)] = jnp.where(low, parts[0], parts[1])
        prev = carried[2 * j : 2 * j + 2].reshape(2 * DIM, STATE)
        cum_grad = cum_grad + head_sums(j, g_f * inner[:, cols_of(j)])
        c_sum = c_sum + nn((pair_cols(tab, ENTRY, j) * g_f).astype(BF16), prev)
    flow = grad_scores.astype(BF16)
    b_part[...] = nn(flow, c[...])
    grad_c[...] = (c_sum + tn(flow, b[...])).astype(BF16)
    cum_part[...] = cum_grad


def inside_grads(x, b, c, rows, tab, carried, inner, grad):
    outs = [
        ((ROWS, WIDE), F32),
        ((ROWS, STATE), BF16),
        ((ROWS, STATE), F32),
        ((HEADS, ROWS), F32),
    ]
    return staged(inside_kernel, (), (x, b, c, rows, tab, carried, inner, grad), outs, 5.0, 60)


def backward_kernel(
    skip, rate, x, b, rows, tab_ref, carried, grad, part, b_part, cum_part, after, grad_x, grad_dt, grad_b
):
    tab = tab_ref[...]
    low = iota((ROWS, 2 * DIM), 1) < DIM
    b_sum = b_part[...]
    step_grad = jnp.zeros((HEADS, ROWS), F32)
    state_dot = jnp.zeros((HEADS, ROWS), F32)
    tail_dot = jnp.zeros((HEADS, ROWS), F32)
    for j in range(PAIRS):
        x_pair = x[:, cols_of(j)].astype(F32)
        step = pair_cols(tab, STEP, j)
        scaled = x_pair * step
        g_f = grad[:, cols_of(j)].astype(F32)
        nxt = after[2 * j : 2 * j + 2].reshape(2 * DIM, STATE)
        prev = carried[2 * j : 2 * j + 2].reshape(2 * DIM, STATE)
        etail = pair_cols(tab, ETAIL, j)
        from_tail = etail * nt(b[...], nxt)
        total = part[:, cols_of(j)] + from_tail
        gain = jnp.where(low, skip[2 * j], skip[2 * j + 1])
        grad_x[:, cols_of(j)] = (step * total + gain * g_f).astype(BF16)
        step_grad = step_grad + head_sums(j, x_pair * total)
        tail_dot = tail_dot + head_sums(j, scaled * from_tail)
        product = nxt.astype(F32) * prev.astype(F32)
        head = iota((HEADS, 2 * DIM), 0)
        own_rows = (head == 2 * j + iota((HEADS, 2 * DIM), 1) // DIM).astype(BF16)
        upper = product.astype(BF16)
        lower = (product - upper.astype(F32)).astype(BF16)
        state_dot = state_dot + nn(own_rows, upper) + nn(own_rows, lower)
        b_sum = b_sum + nn((etail * scaled).astype(BF16), nxt)
    grad_b[...] = b_sum.astype(BF16)
    step_rows = rows[STEP * HEADS : (STEP + 1) * HEADS, :]
    through = rows[THROUGH * HEADS : (THROUGH + 1) * HEADS, :]
    end = jnp.sum(tail_dot, axis=1, keepdims=True) + jnp.sum(
        through * state_dot, axis=1, keepdims=True
    )
    cum_grad = cum_part[...] - step_rows * step_grad
    since = (iota((ROWS, ROWS), 0) >= iota((ROWS, ROWS), 1)).astype(F32)
    decay_grad = dot(cum_grad, since, ((1,), (0,)), HIGHEST) + end
    head = iota((HEADS, ROWS), 0)
    rate_rows = jnp.zeros((HEADS, ROWS), F32)
    for h in range(HEADS):
        rate_rows = jnp.where(head == h, rate[h], rate_rows)
    sig = rows[SIG * HEADS : (SIG + 1) * HEADS, :]
    grad_dt[...] = (step_grad - rate_rows * decay_grad) * sig


def backward(skip, rate, x, b, rows, tab, carried, grad, part, b_part, cum_part, after):
    outs = [((ROWS, WIDE), BF16), ((HEADS, ROWS), F32), ((ROWS, STATE), BF16)]
    arrays = (x, b, rows, tab, carried, grad, part, b_part, cum_part, after)
    return staged(backward_kernel, (skip, rate), arrays, outs, 5.0)


NEAR_FAR = (0, 1, 3, 2)
CHUNKS = 8


def start(*copies):
    for copy in copies:
        copy.start()


def wait(*copies):
    for copy in copies:
        copy.wait()


def paced(loads, ahead=2):
    for batch in loads[:ahead]:
        start(*batch)
    for n, batch in enumerate(loads):
        wait(*batch)
        if n + ahead < len(loads):
            start(*loads[n + ahead])
        yield n


def vmem(n):
    return [pl.BlockSpec(memory_space=pltpu.VMEM)] * n


def project_kernel(
    place, grad_hbm, weight_hbm, mixed, rows, c, keep, send, grad_mix, out, *scratch
):
    grad, weight, ordered, acc, sems = scratch
    plane, core = place[0], place[1]
    planes, _, share, _ = mixed.shape
    tile = weight.shape[1] // CHUNKS
    loads = []
    for n in range(CHUNKS):
        cols = pl.ds(n * tile, tile)
        loads.append(
            (
                pltpu.make_async_copy(grad_hbm.at[:, cols], grad.at[:, cols], sems.at[0, n]),
                pltpu.make_async_copy(weight_hbm.at[:, cols], weight.at[:, cols], sems.at[1, n]),
            )
        )
    for n in paced(loads):
        if n == 0:
            for k, step in enumerate(NEAR_FAR):
                to = (plane + step) % planes
                ordered[k * share : (k + 1) * share] = mixed[to, core]
                ordered[(planes + k) * share : (planes + k + 1) * share] = mixed[to, 1 - core]
        cols = slice(n * tile, (n + 1) * tile)
        part = nt(weight[:, cols], grad[:, cols])
        if n == 0:
            acc[...] = part
        else:
            acc[...] += part
        both = nn(ordered[...], weight[:, cols]).astype(BF16)
        keep[:, :, cols] = both[: planes * share].reshape(planes, share, tile)
        send[:, :, cols] = both[planes * share :].reshape(planes, share, tile)
    for h in range(HEADS):
        part = acc[h * DIM : (h + 1) * DIM].astype(BF16)
        entry = rows[ENTRY * HEADS + h : ENTRY * HEADS + h + 1, :]
        out[h] = nn((part.astype(F32) * entry).astype(BF16), c[...]).astype(BF16)
    for j in range(PAIRS):
        grad_mix[:, cols_of(j)] = acc[cols_of(j)].T.astype(BF16)


def project(place, grad, weight, mixed, rows, c):
    inner, width = weight.shape
    planes, _, share, _ = mixed.shape
    return pl.pallas_call(
        project_kernel,
        in_specs=smem(1) + hbm(2) + vmem(3),
        out_specs=vmem(4),
        out_shape=(
            jax.ShapeDtypeStruct((planes, share, width), BF16),
            jax.ShapeDtypeStruct((planes, share, width), BF16),
            jax.ShapeDtypeStruct((ROWS, inner), BF16),
            jax.ShapeDtypeStruct((HEADS, DIM, STATE), BF16),
        ),
        scratch_shapes=[
            pltpu.VMEM(grad.shape, BF16),
            pltpu.VMEM(weight.shape, BF16),
            pltpu.VMEM((ROWS, inner), BF16),
            pltpu.VMEM((inner, ROWS), F32),
            pltpu.SemaphoreType.DMA((2, CHUNKS)),
        ],
        compiler_params=params(60),
        cost_estimate=took(10.0),
    )(place, *pinned(grad), weight, mixed, rows, c)


def plane_sums(keep, taken, first, rest, outs, combine):
    n = len(first)
    shape = keep.shape[1:]

    def body(*refs):
        a_hbm, b_hbm = refs[:2]
        extra = refs[2 : 2 + len(rest)]
        results = refs[2 + len(rest) : 2 + len(rest) + len(outs)]
        a, b = refs[-3 - len(rest) : -1 - len(rest)]
        local, sems = refs[-1 - len(rest) : -1], refs[-1]
        copies = [
            pltpu.make_async_copy(source, target, sems.at[k])
            for k, (source, target) in enumerate(zip(extra, local, strict=True))
        ]
        for k, plane in enumerate(first):
            for side, (source, target) in enumerate(((a_hbm, a), (b_hbm, b))):
                at = len(rest) + 2 * k + side
                copies.append(pltpu.make_async_copy(source.at[plane], target.at[k], sems.at[at]))
        start(*copies)
        wait(*copies)
        combine(a, b, local, results)

    return pl.pallas_call(
        body,
        in_specs=hbm(2 + len(rest)),
        out_specs=vmem(len(outs)),
        out_shape=tuple(jax.ShapeDtypeStruct(out, BF16) for out in outs),
        scratch_shapes=[pltpu.VMEM((n,) + shape, BF16)] * 2
        + [pltpu.VMEM(r.shape, BF16) for r in rest]
        + [pltpu.SemaphoreType.DMA((len(rest) + 2 * n,))],
        compiler_params=params(),
        cost_estimate=took(1.5),
    )(*pinned(keep, taken, *rest))


def add(*parts):
    total = parts[0].astype(F32)
    for part in parts[1:]:
        total = total + part.astype(F32)
    return total


def far_sums(a, b, rest, results):
    half = a.shape[1] // 2
    for k in range(2):
        rows = slice(k * half, (k + 1) * half)
        results[k][...] = add(a[0, rows], b[0, rows]).astype(BF16)


def near_sums(a, b, rest, results):
    half = a.shape[1] // 2
    for k in range(2):
        for part in range(2):
            rows = slice(part * half, (part + 1) * half)
            extra = (rest[k][...],) if part == k else ()
            results[k][rows] = add(a[k, rows], b[k, rows], *extra).astype(BF16)


def last_sum(a, b, rest, results):
    results[0][...] = add(a[0], b[0], rest[0][...], rest[1][...]).astype(BF16)


def arrange_kernel(place, *refs):
    pieces, result, tokens, out, sems = refs[:8], refs[8], refs[9], refs[10], refs[11]
    slabs, sides, share, cols = tokens.shape
    copies = []
    for side in range(2):
        core = place[1] if side == 0 else 1 - place[1]
        for k, piece in enumerate(pieces[side * 4 : side * 4 + 4]):
            at = 2 * ((place[0] + (0, 3, 1, 2)[k]) % 4) + core
            copies.append(pltpu.make_async_copy(piece, tokens.at[:, at], sems.at[side * 4 + k]))
    for copy in copies:
        copy.start()
    for copy in copies:
        copy.wait()
    wide = sides * share
    stores = []
    for k in range(slabs):
        out[:, k * wide : (k + 1) * wide] = tokens[k].reshape(wide, cols).T
        if k % 4 == 3:
            done = pl.ds((k - 3) * wide, 4 * wide)
            stores.append(
                pltpu.make_async_copy(out.at[:, done], result.at[:, done], sems.at[8 + k // 4])
            )
            start(stores[-1])
    wait(*stores)


def arrange(place, pieces, slabs):
    share = 32
    cols = pieces[0].shape[1]
    views = [p.reshape(-1, share, cols) for p in pieces]
    return pl.pallas_call(
        arrange_kernel,
        in_specs=smem(1) + hbm(len(views)),
        out_specs=hbm(1)[0],
        out_shape=jax.ShapeDtypeStruct((cols, slabs * 8 * share), BF16),
        scratch_shapes=[
            pltpu.VMEM((slabs, 8, share, cols), BF16),
            pltpu.VMEM((cols, slabs * 8 * share), BF16),
            pltpu.SemaphoreType.DMA((len(views) + slabs // 4,)),
        ],
        compiler_params=params(60),
        cost_estimate=took(3.5),
    )(place, *views)


def weight_kernel(left_hbm, right_hbm, out, left, right, acc, sems):
    steps = sems.shape[1]
    tile = left.shape[1] // steps
    spans = [pl.ds(n * tile, tile) for n in range(steps)]
    loads = [
        (
            pltpu.make_async_copy(left_hbm.at[:, span], left.at[:, span], sems.at[0, n]),
            pltpu.make_async_copy(right_hbm.at[span], right.at[span], sems.at[1, n]),
        )
        for n, span in enumerate(spans)
    ]
    for n in paced(loads):
        span = slice(n * tile, (n + 1) * tile)
        part = nn(left[:, span], right[span])
        if n == 0:
            acc[...] = part
        elif n < steps - 1:
            acc[...] += part
        else:
            out[...] = (acc[...] + part).astype(BF16)


def weight_grad(left, right):
    cols, _ = left.shape
    wide = right.shape[1]
    return pl.pallas_call(
        weight_kernel,
        in_specs=hbm(2),
        out_specs=vmem(1)[0],
        out_shape=jax.ShapeDtypeStruct((cols, wide), BF16),
        scratch_shapes=[
            pltpu.VMEM(left.shape, BF16),
            pltpu.VMEM(right.shape, BF16),
            pltpu.VMEM((cols, wide), F32),
            pltpu.SemaphoreType.DMA((2, 4)),
        ],
        compiler_params=params(22),
        cost_estimate=took(7.0),
    )(*pinned(left, right))


SWAP = [(i, i ^ 1) for i in range(8)]


def along_z(d):
    return [(2 * z + c, 2 * ((z + d) % 4) + c) for z in range(4) for c in range(2)]


def after(value, *others):
    return lax.optimization_barrier((value,) + others)[0]


def swap(value):
    return lax.ppermute(value, "tp", SWAP)


def up(value):
    return lax.ppermute(value, "tp", along_z(1))


def down(value):
    return lax.ppermute(value, "tp", along_z(-1))


def over_slabs(value):
    return lax.all_to_all(value, "ctx", 0, 0, tiled=True)


def shards(
    ssm_input,
    dt_raw,
    b_proj,
    c_proj,
    dt_bias,
    decay_rate,
    skip_gain,
    doc_start,
    out_weight,
    grad_out,
):
    share, width = grad_out.shape
    n_ctx = lax.axis_size("ctx")
    tp = lax.axis_index("tp").astype(jnp.int32)
    place = jnp.stack([tp // 2, tp % 2])
    b, c, x, dt, doc, weight = pinned(
        b_proj.reshape(ROWS, STATE),
        c_proj.reshape(ROWS, STATE),
        ssm_input,
        dt_raw.T,
        doc_start.reshape(1, ROWS),
        out_weight,
    )
    bias, rate, skip = pinned(dt_bias, decay_rate, skip_gain)

    grad_full = lax.all_gather(grad_out, "tp", axis=0, tiled=True)
    payload, rows, tab = states(bias, rate, x, dt, doc, b)
    carried, decay = prefix(over_slabs(payload))
    (carried,) = pinned(over_slabs(carried))
    mixed, inner = mixer(skip, x, b, c, rows, tab, carried)
    (inner,) = pinned(inner)
    mixed_all = lax.all_gather(mixed, "ctx", axis=0, tiled=True)
    columns = lax.all_to_all(after(grad_out, decay), "ctx", 1, 0, tiled=True)

    keep, send, grad_mix, local = project(
        place, grad_full, weight, mixed.reshape(4, 2, share, WIDE), rows, c
    )
    local, columns, send = lax.optimization_barrier((local, columns, send))
    c_up, c_down = up(columns), down(columns)
    local = over_slabs(local)
    taken = swap(send)
    half = share // 2
    (grad_mix,) = pinned(grad_mix)
    far = plane_sums(keep, taken, (3,), (), ((half, width),) * 2, far_sums)
    far = up(far[0]), down(far[1])
    next_grad = suffix(local, decay)
    next_grad, grad_mix, c_up, c_down = lax.optimization_barrier(
        (next_grad, grad_mix, c_up, c_down)
    )
    c_far = up(c_up)
    next_grad = over_slabs(next_grad)
    grads = inside_grads(x, b, c, rows, tab, carried, inner, grad_mix)
    grad_c = grads[1]
    next_grad, taken, c_down = lax.optimization_barrier((next_grad, taken, c_down))
    part, b_part, cum_part = pinned(grads[0], grads[2], grads[3])
    near = plane_sums(keep, taken, (1, 2), far, ((share, width),) * 2, near_sums)
    near = up(near[0]), down(near[1])
    mine = (after(columns, taken), c_up, c_down, after(c_far, taken))
    pieces = mine + tuple(swap(piece) for piece in mine)
    left = arrange(place, pieces, n_ctx)
    grad_x, grad_dt, grad_b = backward(
        skip, rate, x, b, rows, tab, carried, grad_mix, part, b_part, cum_part, next_grad
    )
    (layer_out,) = plane_sums(keep, taken, (0,), near, ((share, width),), last_sum)
    weight_sum = weight_grad(left, after(mixed_all, grad_x))
    return (
        layer_out,
        grad_x,
        grad_dt.T,
        grad_b.reshape(ROWS, 1, STATE),
        grad_c.reshape(ROWS, 1, STATE),
        weight_sum,
    )


def solution(mesh):
    in_specs = (
        P("ctx", "tp"),
        P("ctx", "tp"),
        P("ctx", "tp", None),
        P("ctx", "tp", None),
        P("tp"),
        P("tp"),
        P("tp"),
        P("ctx"),
        P("tp", None),
        P(("ctx", "tp"), None),
    )
    out_specs = (
        P(("ctx", "tp"), None),
        P("ctx", "tp"),
        P("ctx", "tp"),
        P("ctx", "tp", None),
        P("ctx", "tp", None),
        P("ctx", "tp"),
    )
    return jax.shard_map(shards, mesh=mesh, in_specs=in_specs, out_specs=out_specs, check_vma=False)
```
